32 devices in a mesh: grid: 4 (over x, core), comp: 8 (over z, y).
Axes of the slice: x: 2, y: 2, z: 4, core: 2. Of those that a mesh axis runs over, the one named last changes fastest.
Arguments:
- spectra: float32 [32, 32, 36, 2048], P('comp', None, None, 'grid'), may hold values from 0.1 to 2
- u_wind: float32 [32, 2048], P(None, 'grid'), may hold values from 2 to 20
- wind_dir: float32 [32, 2048], P(None, 'grid'), may hold values from -3.140625 to 3.140625
- sea_mask: int32 [32, 2048], P(None, 'grid'), may hold values from 0 to 1, as said below
Outputs:
- spectra_next: float32 [32, 32, 36, 2048], P('comp', None, None, 'grid')
The draws below stay inside these ranges and needn't reach their ends.
Inputs may be any that keep to these rules, and one draw needn't show every extreme that they name: sea_mask is 1 at sea and 0 on land; land lies in rectangular blocks of rows and columns.
All inputs are finite; a program needn't handle non-finite values.
Results may differ from the reference program's by a relative error of at most 0.00016.
Values sent between devices are 32-bit elements; how exact they have to be, the bound alone decides.
No kernel may reach another device: no remote copies, remote signals or barrier semaphores. Data moves between devices by JAX's collectives and lax.ppermute only.
A program may use at most 192 MiB of HBM per device.

```python
import math
import jax
import jax.numpy as jnp
from jax import lax

NK = 32
NTH = 36
LAT = 32
NLON = 2048


def draw_sea_mask(key, part):
    block_count = max(4, NLON // 16)
    keys = jax.random.split(key, 4)
    top_row = jax.random.randint(keys[0], (block_count, 1, 1), 0, LAT)
    height = jax.random.randint(keys[1], (block_count, 1, 1), 2, LAT // 2 + 3)
    left_col = jax.random.randint(keys[2], (block_count, 1, 1), 0, NLON)
    breadth = jax.random.randint(keys[3], (block_count, 1, 1), 3, 41)
    row_index = jnp.arange(LAT, dtype=jnp.int32)[None, :, None]
    col_index = jnp.arange(NLON, dtype=jnp.int32)[None, None, :]
    inside = (row_index >= top_row) & (row_index < top_row + height) & (col_index >= left_col) & (col_index < left_col + breadth)
    land_cells = jnp.any(inside, axis=0)
    return jnp.where(land_cells, 0, 1).astype(jnp.int32)


def block_scale(key, shape, cuts, low, high):
    level, own = 1.0, jax.random.fold_in(key, 6)
    for axis_at, blocks in cuts:
        heights = jnp.exp(jax.random.uniform(jax.random.fold_in(own, axis_at), (blocks,), jnp.float32, low / len(cuts), high / len(cuts)))
        level = level * jnp.repeat(heights, shape[axis_at] // blocks).reshape([-1 if axis == axis_at else 1 for axis in range(len(shape))])
    return level


def setup_inputs(seed: int = 0) -> dict:
    streams_of = jax.random.split(jax.random.key(seed), 5)
    return {
        "spectra": jnp.clip(jnp.exp(math.log(2.0) - 2.9957323 * jax.random.uniform(streams_of[0], (NK, LAT, NTH, NLON), jnp.float32) ** block_scale(streams_of[0], (NK, LAT, NTH, NLON), ((0, 8), (3, 4)), -0.2, 0.2)), 0.1, 2.0),
        "u_wind": jnp.clip(2.0 + 18.0 * jax.random.uniform(streams_of[1], (LAT, NLON), jnp.float32) ** block_scale(streams_of[1], (LAT, NLON), ((1, 4),), -0.2, 0.2), 2.0, 20.0),
        "wind_dir": jnp.clip(jax.random.uniform(streams_of[2], (LAT, NLON), jnp.float32, -3.140625, 3.140625), -3.140625, 3.140625),
        "sea_mask": draw_sea_mask(jax.random.fold_in(streams_of[4], 71), 0),
    }


GRAVITY = 9.81
FREQ_LOW = 0.04
FREQ_RATIO = 1.1
LAMBDA = 0.25
SOURCE_STEP = 120.0
ADVECT_STEP = 220.0
WIND_FACTOR = 3.125e-4
TRANSFER_FACTOR = 0.1
EARTH_RADIUS = 6.371e6
BAND_CENTRE = 30.0
CELL_DEGREES = 0.05
CELL_RADIANS = CELL_DEGREES * math.pi / 180.0
ANGLE_NEAR = 11.48
ANGLE_FAR = 33.56
FREQ_UPPER_SHIFT = math.log(1.0 + LAMBDA) / math.log(FREQ_RATIO)
FREQ_LOWER_SHIFT = math.log(1.0 - LAMBDA) / math.log(FREQ_RATIO)
WEIGHT_UPPER = 1.0 / (1.0 + LAMBDA) ** 4
WEIGHT_LOWER = 1.0 / (1.0 - LAMBDA) ** 4
WEIGHT_CROSS = 2.0 / (1.0 - LAMBDA * LAMBDA) ** 4
HIGHEST = lax.Precision.HIGHEST


def hat_matrix(bin_count, bin_shift, periodic):
    target = jnp.arange(bin_count, dtype=jnp.float32)[:, None] + bin_shift
    source = jnp.arange(bin_count, dtype=jnp.float32)[None, :]
    offset_gap = target - source
    if periodic:
        offset_gap = jnp.mod(offset_gap + bin_count / 2.0, float(bin_count)) - bin_count / 2.0
    return jnp.maximum(0.0, 1.0 - jnp.abs(offset_gap))


def nonlinear(point_block):
    freq_count = point_block.shape[0]
    dir_count = point_block.shape[2]
    freq_upper = hat_matrix(freq_count, FREQ_UPPER_SHIFT, False)
    freq_lower = hat_matrix(freq_count, FREQ_LOWER_SHIFT, False)
    spread_upper = jnp.einsum("km,mrjq->krjq", freq_upper, point_block, precision=HIGHEST)
    spread_lower = jnp.einsum("km,mrjq->krjq", freq_lower, point_block, precision=HIGHEST)
    near_bins = ANGLE_NEAR * dir_count / 360.0
    far_bins = ANGLE_FAR * dir_count / 360.0
    squared = point_block * point_block
    centre_total = jnp.zeros_like(point_block)
    back_upper = jnp.zeros_like(point_block)
    back_lower = jnp.zeros_like(point_block)
    for shifts in ((near_bins, -far_bins), (-near_bins, far_bins)):
        dir_upper = hat_matrix(dir_count, shifts[0], True)
        dir_lower = hat_matrix(dir_count, shifts[1], True)
        plus_value = jnp.einsum("jn,krnq->krjq", dir_upper, spread_upper, precision=HIGHEST)
        minus_value = jnp.einsum("jn,krnq->krjq", dir_lower, spread_lower, precision=HIGHEST)
        interaction = TRANSFER_FACTOR * (squared * (plus_value * WEIGHT_UPPER + minus_value * WEIGHT_LOWER)
                                         - WEIGHT_CROSS * point_block * plus_value * minus_value)
        centre_total = centre_total - 2.0 * interaction
        back_upper = back_upper + jnp.einsum("jn,krjq->krnq", dir_upper, interaction, precision=HIGHEST)
        back_lower = back_lower + jnp.einsum("jn,krjq->krnq", dir_lower, interaction, precision=HIGHEST)
    centre_total = centre_total + jnp.einsum("km,krjq->mrjq", freq_upper, back_upper, precision=HIGHEST)
    return centre_total + jnp.einsum("km,krjq->mrjq", freq_lower, back_lower, precision=HIGHEST)


def frequency(freq_index):
    return (FREQ_LOW * jnp.power(FREQ_RATIO, freq_index.astype(jnp.float32))).reshape(-1, 1, 1, 1)


def wind_growth(freq, angles, wind_speed, heading):
    radian_freq = 2.0 * math.pi * freq
    celerity = GRAVITY / radian_freq
    alignment = jnp.cos(angles) * jnp.cos(heading) + jnp.sin(angles) * jnp.sin(heading)
    return WIND_FACTOR * SOURCE_STEP * radian_freq * jnp.maximum(0.0, wind_speed / celerity * alignment - 1.0)


def courant_x(freq, angles, row_index, total_rows):
    group_speed = GRAVITY / (4.0 * math.pi * freq)
    latitude = BAND_CENTRE + (row_index.astype(jnp.float32) - (total_rows - 1) / 2.0) * CELL_DEGREES
    row_cos = jnp.cos(latitude * (math.pi / 180.0)).reshape(1, -1, 1, 1)
    return group_speed * jnp.cos(angles) * ADVECT_STEP / (EARTH_RADIUS * row_cos * CELL_RADIANS)


def courant_y(freq, angles):
    group_speed = GRAVITY / (4.0 * math.pi * freq)
    return group_speed * jnp.sin(angles) * ADVECT_STEP / (EARTH_RADIUS * CELL_RADIANS)


def latitude_cos(total_rows):
    cell_lat = BAND_CENTRE + (jnp.arange(total_rows, dtype=jnp.float32) - (total_rows - 1) / 2.0) * CELL_DEGREES
    face_lat = BAND_CENTRE + (jnp.arange(total_rows + 1, dtype=jnp.float32) - total_rows / 2.0) * CELL_DEGREES
    cell_cos = jnp.cos(cell_lat * (math.pi / 180.0)).reshape(1, -1, 1, 1)
    face_cos = jnp.cos(face_lat * (math.pi / 180.0)).reshape(1, -1, 1, 1)
    return face_cos, 1.0 / cell_cos


def advect(padded, courant, face_weight, cell_weight, along_axis):
    cells = padded.shape[along_axis] - 4

    def piece_at(offset_cells, length_cells):
        return lax.slice_in_dim(padded, offset_cells, offset_cells + length_cells, axis=along_axis)

    left_cell = piece_at(1, cells + 1)
    right_cell = piece_at(2, cells + 1)
    far_left = piece_at(0, cells + 1)
    far_right = piece_at(3, cells + 1)
    curvature = jnp.where(courant >= 0.0, right_cell - 2.0 * left_cell + far_left,
                          far_right - 2.0 * right_cell + left_cell)
    face_value = 0.5 * (left_cell + right_cell) - 0.5 * courant * (right_cell - left_cell) \
        - (1.0 - courant * courant) / 6.0 * curvature
    flux_face = courant * face_value * face_weight
    difference = lax.slice_in_dim(flux_face, 1, cells + 1, axis=along_axis) - lax.slice_in_dim(flux_face, 0, cells, axis=along_axis)
    return piece_at(2, cells) - difference * cell_weight


def reference(spectra, u_wind, wind_dir, sea_mask):
    mask_field = sea_mask.astype(jnp.float32)[None, :, None, :]
    masked = spectra * mask_field
    freq = frequency(jnp.arange(NK, dtype=jnp.int32))
    angles = (jnp.arange(NTH, dtype=jnp.float32) * (2.0 * math.pi / NTH)).reshape(1, 1, -1, 1)
    growth = wind_growth(freq, angles, u_wind[None, :, None, :], wind_dir[None, :, None, :])
    block_width = math.gcd(NLON, 256)
    block_total = NLON // block_width
    stacked = jnp.moveaxis(masked.reshape(NK, LAT, NTH, block_total, block_width), 3, 0)
    pieces = lax.map(nonlinear, stacked)
    increment = jnp.moveaxis(pieces, 0, 3).reshape(NK, LAT, NTH, NLON)
    post = masked * (1.0 + growth) + increment
    padded = jnp.pad(post, ((0, 0), (0, 0), (0, 0), (2, 2)))
    crossing = courant_x(freq, angles, jnp.arange(LAT, dtype=jnp.int32), LAT)
    swept_x = advect(padded, crossing, 1.0, 1.0, 3) * mask_field
    padded_rows = jnp.pad(swept_x, ((0, 0), (2, 2), (0, 0), (0, 0)))
    face_cos, cell_inverse = latitude_cos(LAT)
    return advect(padded_rows, courant_y(freq, angles), face_cos, cell_inverse, 1) * mask_field
```

```python
import functools
import math

import jax
import jax.numpy as jnp
import numpy as np
from jax import lax
from jax.experimental import pallas as pl
from jax.experimental.pallas import tpu as pltpu
from jax.sharding import PartitionSpec as P

GRAVITY = 9.81
FREQ_LOW = 0.04
FREQ_RATIO = 1.1
LAMBDA = 0.25
SOURCE_STEP = 120.0
ADVECT_STEP = 220.0
WIND_FACTOR = 0.0003125
TRANSFER_FACTOR = 0.1
EARTH_RADIUS = 6371000.0
BAND_CENTRE = 30.0
CELL_DEGREES = 0.05
CELL_RADIANS = CELL_DEGREES * math.pi / 180.0
ANGLE_NEAR = 11.48
ANGLE_FAR = 33.56
FREQ_UPPER_SHIFT = math.log(1.0 + LAMBDA) / math.log(FREQ_RATIO)
FREQ_LOWER_SHIFT = math.log(1.0 - LAMBDA) / math.log(FREQ_RATIO)
WEIGHT_UPPER = 1.0 / (1.0 + LAMBDA) ** 4
WEIGHT_LOWER = 1.0 / (1.0 - LAMBDA) ** 4
WEIGHT_CROSS = 2.0 / (1.0 - LAMBDA * LAMBDA) ** 4

LANES = 128
VMEM_LIMIT = 60 * 1024 * 1024


def taps(shift):
    low = math.floor(shift)
    part = shift - low
    return ((low, 1.0 - part), (low + 1, part))


UP_TAPS = taps(FREQ_UPPER_SHIFT)
DOWN_TAPS = taps(FREQ_LOWER_SHIFT)
REACH_HIGH = UP_TAPS[1][0]
REACH_LOW = -DOWN_TAPS[0][0]
REACH = REACH_HIGH + REACH_LOW


def pick(values, index):
    chosen = values[0]
    for place in range(1, len(values)):
        chosen = jnp.where(index == place, values[place], chosen)
    return chosen


def sub_rows(rows):
    return 8 if rows % 8 == 0 else rows


def pack_kernel(parts, rows, spot_ref, x_ref, mask_ref, *outs):
    spot = spot_ref[0]
    mask = mask_ref[...].astype(jnp.float32)
    blocks = [
        x_ref[0, :, b * rows : (b + 1) * rows, :] * mask[None, b * rows : (b + 1) * rows, :]
        for b in range(parts)
    ]
    for turn in range(parts):
        outs[turn][0] = pick(blocks, lax.rem(spot + turn, parts))


def pack(spot, spectra, sea_mask, column, parts):
    freqs, dirs, total_rows, _ = spectra.shape
    rows = total_rows // parts
    shape = jax.ShapeDtypeStruct((freqs, dirs, rows, LANES), jnp.float32)
    return pl.pallas_call(
        functools.partial(pack_kernel, parts, rows),
        out_shape=[shape] * parts,
        grid_spec=pltpu.PrefetchScalarGridSpec(
            num_scalar_prefetch=1,
            grid=(freqs,),
            in_specs=[
                pl.BlockSpec((1, dirs, total_rows, LANES), lambda f, s: (f, 0, 0, column)),
                pl.BlockSpec((total_rows, LANES), lambda f, s: (0, column)),
            ],
            out_specs=[pl.BlockSpec((1, dirs, rows, LANES), lambda f, s: (f, 0, 0, 0))] * parts,
        ),
        compiler_params=pltpu.CompilerParams(vmem_limit_bytes=VMEM_LIMIT),
        name=f"pack_{column}",
    )(spot, spectra, sea_mask)


def source_kernel(
    parts,
    freqs,
    dirs,
    rows,
    spot_ref,
    gain_ref,
    drop_ref,
    along_ref,
    across_ref,
    *refs,
):
    count = 3 * parts
    ins, outs = refs[:count], refs[count : count + parts]
    window, wind, back_up, back_down, centre, post, in_sems, out_sems = refs[count + parts :]
    spot = spot_ref[0]
    first = spot_ref[1]
    span = parts * freqs
    step = sub_rows(rows)
    pieces = rows // step

    def block_of(turn):
        return lax.rem(spot + parts - turn, parts)

    def fetches(piece):
        copies = []
        for group in range(3):
            for turn in range(parts):
                place = (group * parts + block_of(turn)) * freqs
                copies.append(
                    pltpu.make_async_copy(
                        ins[group * parts + turn].at[:, :, pl.ds(piece * step, step), :],
                        window.at[piece, pl.ds(place, freqs)],
                        in_sems.at[piece, group * parts + turn],
                    )
                )
        return copies

    def stores(piece):
        copies = []
        for turn in range(parts):
            copies.append(
                pltpu.make_async_copy(
                    post.at[piece, pl.ds(block_of(turn) * freqs, freqs)],
                    outs[turn].at[:, :, pl.ds(piece * step, step), :],
                    out_sems.at[piece, turn],
                )
            )
        return copies

    for piece in range(pieces):
        for copy in fetches(piece):
            copy.start()

    scale_up = TRANSFER_FACTOR * WEIGHT_UPPER
    scale_down = TRANSFER_FACTOR * WEIGHT_LOWER
    cross = TRANSFER_FACTOR * WEIGHT_CROSS / (scale_up * scale_down)
    near = taps(ANGLE_NEAR * dirs / 360.0)
    far = taps(ANGLE_FAR * dirs / 360.0)

    along = [along_ref[b * rows : (b + 1) * rows, :] for b in range(parts)]
    across = [across_ref[b * rows : (b + 1) * rows, :] for b in range(parts)]
    along = pick(along, spot)
    across = pick(across, spot)

    for piece in range(pieces):
        low = piece * step
        for j in range(dirs):
            angle = 2.0 * math.pi * j / dirs
            wind[j] = (
                along[low : low + step] * math.cos(angle)
                + across[low : low + step] * math.sin(angle)
            )
        for copy in fetches(piece):
            copy.wait()

        def delta_step(index, carry):
            k = span - REACH_HIGH + index

            @functools.cache
            def energy(j):
                return window[piece, k, j]

            @functools.cache
            def upper(j):
                (o0, w0), (o1, w1) = UP_TAPS
                return (scale_up * w0) * window[piece, k + o0, j] + (scale_up * w1) * window[
                    piece, k + o1, j
                ]

            @functools.cache
            def lower(j):
                (o0, w0), (o1, w1) = DOWN_TAPS
                return (scale_down * w0) * window[piece, k + o0, j] + (scale_down * w1) * window[
                    piece, k + o1, j
                ]

            @functools.cache
            def delta(sign, j):
                plus = sum(w * upper((j + sign * o) % dirs) for o, w in near)
                minus = sum(w * lower((j - sign * o) % dirs) for o, w in far)
                value = energy(j)
                return value * (value * (plus + minus) - cross * (plus * minus))

            for j in range(dirs):
                back_up[index, j] = sum(
                    w * (delta(1, (j - o) % dirs) + delta(-1, (j + o) % dirs)) for o, w in near
                )
                back_down[index, j] = sum(
                    w * (delta(1, (j + o) % dirs) + delta(-1, (j - o) % dirs)) for o, w in far
                )
                centre[index, j] = -2.0 * (delta(1, j) + delta(-1, j))
            return carry

        lax.fori_loop(0, span + REACH, delta_step, 0)

        def out_step(m, carry):
            gain = gain_ref[first + m]
            drop = drop_ref[first + m]
            index = m + REACH_HIGH
            for j in range(dirs):
                value = window[piece, span + m, j]
                total = value * (1.0 + jnp.maximum(0.0, gain * wind[j] - drop)) + centre[index, j]
                for o, w in UP_TAPS:
                    total = total + w * back_up[index - o, j]
                for o, w in DOWN_TAPS:
                    total = total + w * back_down[index - o, j]
                post[piece, m, j] = total
            return carry

        lax.fori_loop(0, span, out_step, 0)
        for copy in stores(piece):
            copy.start()
    for piece in range(pieces):
        for copy in stores(piece):
            copy.wait()


def source(scalars, gain, drop, along, across, held, below, above, column):
    parts = len(held)
    freqs, dirs, rows, _ = held[0].shape
    total_rows = rows * parts
    span = parts * freqs
    step = sub_rows(rows)
    pieces = rows // step
    shape = jax.ShapeDtypeStruct((freqs, dirs, rows, LANES), jnp.float32)
    smem = pl.BlockSpec(memory_space=pltpu.SMEM)
    anywhere = pl.BlockSpec(memory_space=pl.ANY)
    wind_spec = pl.BlockSpec((total_rows, LANES), lambda i: (0, column))
    inner = (dirs, step, LANES)
    return pl.pallas_call(
        functools.partial(source_kernel, parts, freqs, dirs, rows),
        out_shape=[shape] * parts,
        grid=(1,),
        in_specs=[smem, smem, smem, wind_spec, wind_spec] + [anywhere] * (3 * parts),
        out_specs=[anywhere] * parts,
        scratch_shapes=[
            pltpu.VMEM((pieces, 3 * span) + inner, jnp.float32),
            pltpu.VMEM(inner, jnp.float32),
            pltpu.VMEM((span + REACH,) + inner, jnp.float32),
            pltpu.VMEM((span + REACH,) + inner, jnp.float32),
            pltpu.VMEM((span + REACH,) + inner, jnp.float32),
            pltpu.VMEM((pieces, span) + inner, jnp.float32),
            pltpu.SemaphoreType.DMA((pieces, 3 * parts)),
            pltpu.SemaphoreType.DMA((pieces, parts)),
        ],
        compiler_params=pltpu.CompilerParams(vmem_limit_bytes=VMEM_LIMIT),
        name=f"source_{column}",
    )(scalars, gain, drop, along, across, *below, *held, *above)


def face_weights(courant, forward):
    curve = (courant * courant - 1.0) * (1.0 / 6.0)
    half = 0.5 * courant
    if forward:
        return (courant * curve, courant * (0.5 + half - 2.0 * curve), courant * (0.5 - half + curve))
    return (courant * (0.5 + half + curve), courant * (0.5 - half - 2.0 * curve), courant * curve)


def arc(values):
    count = len(values)
    flags = [value >= 0.0 for value in values]
    starts = [j for j in range(count) if flags[j] and not flags[j - 1]]
    start = starts[0]
    return start, sum(flags)


def sweep_kernel(parts, tiles, dirs, rows, spot_ref, speed_ref, cos_ref, sin_ref, geo_ref, mask_ref, *refs):
    count = parts * (tiles + 2)
    ins, out_ref, wide = refs[:count], refs[count], refs[count + 1]
    spot = spot_ref[0]
    first = spot_ref[2]
    total_rows = rows * parts
    width = tiles * LANES
    speed = speed_ref[first + pl.program_id(0)]
    for tile in range(tiles + 2):
        pieces = [ins[tile * parts + turn][0] for turn in range(parts)]
        for b in range(parts):
            wide[:, b * rows : (b + 1) * rows, tile * LANES : (tile + 1) * LANES] = pick(
                pieces, lax.rem(b + parts - spot, parts)
            )
    mask = mask_ref[...].astype(jnp.float32)
    inverse = geo_ref[0]
    ahead = geo_ref[1]
    behind = geo_ref[2]
    row = lax.broadcasted_iota(jnp.int32, (total_rows, width), 0)

    def repeat(vector):
        return jnp.concatenate([vector] * tiles, axis=1)

    ahead_wide, behind_wide = repeat(ahead), repeat(behind)

    def down(value, amount):
        rolled = pltpu.roll(value, amount % total_rows, axis=0)
        keep = row >= amount if amount > 0 else row < total_rows + amount
        return jnp.where(keep, rolled, 0.0)

    def one(j, forward, northward):
        full = wide[j]
        size = width + 2 * LANES
        weights = face_weights((speed * cos_ref[j]) * inverse, forward)
        step_at = full - pltpu.roll(full, 1, axis=1)
        next_step = pltpu.roll(step_at, size - 1, axis=1)
        if forward:
            steps = (pltpu.roll(step_at, 1, axis=1), step_at, next_step)
        else:
            steps = (step_at, next_step, pltpu.roll(step_at, size - 2, axis=1))
        swept = full[:, LANES : LANES + width]
        for weight, value in zip(weights, steps):
            swept = swept - repeat(weight) * value[:, LANES : LANES + width]
        swept = swept * mask
        low, mid, high = face_weights(speed * sin_ref[j], northward)
        under, over = down(swept, 1), down(swept, -1)
        if northward:
            front = low * under + mid * swept + high * over
            rear = low * down(swept, 2) + mid * under + high * swept
        else:
            front = low * swept + mid * over + high * down(swept, -2)
            rear = low * under + mid * swept + high * over
        out_ref[0, j] = (swept - ahead_wide * front + behind_wide * rear) * mask

    angles = [2.0 * math.pi * j / dirs for j in range(dirs)]
    east = arc([round(math.cos(angle), 12) for angle in angles])
    north = arc([round(math.sin(angle), 12) for angle in angles])

    def member(run, j):
        return (j - run[0]) % dirs < run[1]

    kinds = [(member(east, j), member(north, j)) for j in range(dirs)]
    begin = 0
    while begin < dirs:
        end = begin
        while end < dirs and kinds[end] == kinds[begin]:
            end += 1
        kind = kinds[begin]

        def body(j, carry, kind=kind):
            one(j, *kind)
            return carry

        lax.fori_loop(begin, end, body, 0)
        begin = end


def sweep(scalars, speed, cosines, sines, geometry, sea_mask, chunks, left, right):
    tiles, parts = len(chunks), len(left)
    freqs, dirs, rows, _ = left[0].shape
    total_rows = rows * parts
    width = tiles * LANES
    operands = list(left)
    for tile in chunks:
        operands += tile
    operands += right
    smem = pl.BlockSpec(memory_space=pltpu.SMEM)
    block = pl.BlockSpec((1, dirs, rows, LANES), lambda f: (f, 0, 0, 0))
    return pl.pallas_call(
        functools.partial(sweep_kernel, parts, tiles, dirs, rows),
        out_shape=jax.ShapeDtypeStruct((freqs, dirs, total_rows, width), jnp.float32),
        grid=(freqs,),
        in_specs=[smem] * 4
        + [
            pl.BlockSpec((3, total_rows, LANES), lambda f: (0, 0, 0)),
            pl.BlockSpec((total_rows, width), lambda f: (0, 0)),
        ]
        + [block] * len(operands),
        out_specs=pl.BlockSpec((1, dirs, total_rows, width), lambda f: (f, 0, 0, 0)),
        scratch_shapes=[pltpu.VMEM((dirs, total_rows, width + 2 * LANES), jnp.float32)],
        compiler_params=pltpu.CompilerParams(vmem_limit_bytes=VMEM_LIMIT),
        name="sweep",
    )(scalars, speed, cosines, sines, geometry, sea_mask, *operands)


def group_size(comp_count, freq_local, band_rows):
    for parts in range(1, comp_count + 1):
        if comp_count % parts == 0 and band_rows % parts == 0 and parts * freq_local >= REACH:
            return parts
    return comp_count


def shards(spectra, u_wind, wind_dir, sea_mask):
    freq_local, band_rows, dir_count, lon_cells = spectra.shape
    comp_count = lax.axis_size("comp")
    grid_count = lax.axis_size("grid")
    parts = group_size(comp_count, freq_local, band_rows)
    comp_index = lax.axis_index("comp")
    spot = lax.rem(comp_index, parts)
    first = (comp_index - spot) * freq_local
    scalars = jnp.stack([spot, first, comp_index * freq_local]).astype(jnp.int32)

    turns = []
    for turn in range(parts):
        turns.append(
            [(i, i - i % parts + (i % parts + turn) % parts) for i in range(comp_count)]
        )
    returns = [[(target, origin) for origin, target in pairs] for pairs in turns]
    upward = [(i, i + parts) for i in range(comp_count - parts)]
    downward = [(i + parts, i) for i in range(comp_count - parts)]
    eastward = [(i, i + 1) for i in range(grid_count - 1)]
    westward = [(i + 1, i) for i in range(grid_count - 1)]

    omega = 2.0 * math.pi * FREQ_LOW * FREQ_RATIO ** np.arange(freq_local * comp_count)
    factor = WIND_FACTOR * SOURCE_STEP
    gain = jnp.asarray(factor * omega * omega / GRAVITY, jnp.float32)
    drop = jnp.asarray(factor * omega, jnp.float32)
    speed = jnp.asarray(
        GRAVITY / (2.0 * omega) * ADVECT_STEP / (EARTH_RADIUS * CELL_RADIANS), jnp.float32
    )
    angles = 2.0 * math.pi * np.arange(dir_count) / dir_count
    cosines = jnp.asarray(np.cos(angles), jnp.float32)
    sines = jnp.asarray(np.sin(angles), jnp.float32)
    cells = np.cos(
        np.radians(BAND_CENTRE + (np.arange(band_rows) - (band_rows - 1) / 2.0) * CELL_DEGREES)
    )
    faces = np.cos(
        np.radians(BAND_CENTRE + (np.arange(band_rows + 1) - band_rows / 2.0) * CELL_DEGREES)
    )
    geometry = np.stack([1.0 / cells, faces[1:] / cells, faces[:-1] / cells])
    geometry = jnp.asarray(np.repeat(geometry[:, :, None], LANES, axis=2), jnp.float32)

    along = u_wind * jnp.cos(wind_dir)
    across = u_wind * jnp.sin(wind_dir)

    field = jnp.transpose(spectra, (0, 2, 1, 3))
    tiles = lon_cells // LANES
    order = [tiles - 1] + list(range(tiles - 1))
    chunks = [None] * tiles
    left = right = None
    for column in order:
        packed = pack(scalars, field, sea_mask, column, parts)
        held = [packed[0]] + [
            lax.ppermute(packed[turn], "comp", turns[turn]) for turn in range(1, parts)
        ]
        below = [lax.ppermute(value, "comp", upward) for value in held]
        above = [lax.ppermute(value, "comp", downward) for value in held]
        post = source(scalars, gain, drop, along, across, held, below, above, column)
        chunks[column] = [post[0]] + [
            lax.ppermute(post[turn], "comp", returns[turn]) for turn in range(1, parts)
        ]
        if column == tiles - 1:
            left = [lax.ppermute(value, "grid", eastward) for value in chunks[column]]
        if column == 0:
            right = [lax.ppermute(value, "grid", westward) for value in chunks[column]]
    result = sweep(scalars, speed, cosines, sines, geometry, sea_mask, chunks, left, right)
    return jnp.transpose(result, (0, 2, 1, 3))


def solution(mesh):
    return jax.shard_map(
        shards,
        mesh=mesh,
        in_specs=(P("comp", None, None, "grid"), P(None, "grid"), P(None, "grid"), P(None, "grid")),
        out_specs=P("comp", None, None, "grid"),
        check_vma=False,
    )
```

```python
import functools
import math

import jax
import jax.numpy as jnp
import numpy as np
from jax import lax
from jax.experimental import pallas as pl
from jax.experimental.pallas import tpu as pltpu
from jax.sharding import PartitionSpec as P


GRAVITY = 9.81
FREQ_LOW = 0.04
FREQ_RATIO = 1.1
LAMBDA = 0.25
SOURCE_STEP = 120.0
ADVECT_STEP = 220.0
WIND_FACTOR = 0.0003125
TRANSFER_FACTOR = 0.1
EARTH_RADIUS = 6371000.0
BAND_CENTRE = 30.0
CELL_DEGREES = 0.05
CELL_RADIANS = CELL_DEGREES * math.pi / 180.0
ANGLE_NEAR = 11.48
ANGLE_FAR = 33.56
FREQ_UPPER_SHIFT = math.log(1.0 + LAMBDA) / math.log(FREQ_RATIO)
FREQ_LOWER_SHIFT = math.log(1.0 - LAMBDA) / math.log(FREQ_RATIO)
WEIGHT_UPPER = 1.0 / (1.0 + LAMBDA) ** 4
WEIGHT_LOWER = 1.0 / (1.0 - LAMBDA) ** 4
WEIGHT_CROSS = 2.0 / (1.0 - LAMBDA * LAMBDA) ** 4

LANES = 128
VMEM_LIMIT = 60 * 1024 * 1024


def taps(shift):
    low = math.floor(shift)
    part = shift - low
    return ((low, 1.0 - part), (low + 1, part))


UP_TAPS = taps(FREQ_UPPER_SHIFT)
DOWN_TAPS = taps(FREQ_LOWER_SHIFT)
REACH_HIGH = UP_TAPS[1][0]
REACH_LOW = -DOWN_TAPS[0][0]
REACH = REACH_HIGH + REACH_LOW


def pick(values, index):
    chosen = values[0]
    for place in range(1, len(values)):
        chosen = jnp.where(index == place, values[place], chosen)
    return chosen


def sub_rows(rows):
    return 8 if rows % 8 == 0 else rows


SPOT, GROUP_FIRST, OWN_FIRST, EVEN, HAS_BELOW, HAS_ABOVE = range(6)
BELOW, HERE, ABOVE = range(3)


def pack_kernel(parts, rows, low, size, lean, scalars, x_ref, mask_ref, *outs):
    spot = scalars[SPOT]
    mask = mask_ref[...].astype(jnp.float32)
    starts = [b * rows + low for b in range(parts)]
    freqs = x_ref.shape[0]
    for f in range(freqs):
        blocks = [x_ref[f, :, s : s + size, :] * mask[None, s : s + size, :] for s in starts]
        for turn in range(parts):
            outs[turn][f] = pick(blocks, lax.rem(spot + turn, parts))
    if lean:
        even = scalars[EVEN]
        outs[parts][...] = outs[0][pl.ds(even, freqs - 1)]
        outs[parts + 1][...] = outs[0][pl.ds(1 - even, freqs - 1)]


def pack(scalars, spectra, sea_mask, chunk, parts, lean):
    column, low, size = chunk
    freqs, dirs, total_rows, _ = spectra.shape
    rows = total_rows // parts

    def shape(count):
        return jax.ShapeDtypeStruct((count, dirs, size, LANES), jnp.float32)

    counts = [freqs] * parts + [freqs - 1] * (2 if lean else 0)
    return pl.pallas_call(
        functools.partial(pack_kernel, parts, rows, low, size, lean),
        out_shape=[shape(count) for count in counts],
        grid=(1,),
        in_specs=[
            pl.BlockSpec(memory_space=pltpu.SMEM),
            pl.BlockSpec((freqs, dirs, total_rows, LANES), lambda i: (0, 0, 0, column)),
            pl.BlockSpec((total_rows, LANES), lambda i: (0, column)),
        ],
        out_specs=[
            pl.BlockSpec((count, dirs, size, LANES), lambda i: (0, 0, 0, 0)) for count in counts
        ],
        compiler_params=pltpu.CompilerParams(vmem_limit_bytes=VMEM_LIMIT),
    )(scalars, spectra, sea_mask)


def join_kernel(freqs, scalars, own_ref, other_ref, a_ref, b_ref, sems):
    even, spot = scalars[EVEN], scalars[SPOT]
    for side, (out_ref, up) in enumerate(((a_ref, even), (b_ref, 1 - even))):
        rest = pltpu.make_async_copy(
            other_ref.at[pl.ds(up, freqs - 1)], out_ref.at[pl.ds(up, freqs - 1)], sems.at[side, 0]
        )
        rest.start()
        place = (1 - up) * (freqs - 1)
        from_own = spot == up

        @pl.when(from_own)
        def _():
            pltpu.make_async_copy(own_ref.at[place], out_ref.at[place], sems.at[side, 1]).start()

        @pl.when(jnp.logical_not(from_own))
        def _():
            pltpu.make_async_copy(other_ref.at[place], out_ref.at[place], sems.at[side, 1]).start()

    for side, out_ref in enumerate((a_ref, b_ref)):
        pltpu.make_async_copy(
            other_ref.at[pl.ds(0, freqs - 1)], out_ref.at[pl.ds(0, freqs - 1)], sems.at[side, 0]
        ).wait()
        pltpu.make_async_copy(other_ref.at[0], out_ref.at[0], sems.at[side, 1]).wait()


def join(scalars, own, other):
    anywhere = pl.BlockSpec(memory_space=pl.ANY)
    shape = jax.ShapeDtypeStruct(own.shape, own.dtype)
    return pl.pallas_call(
        functools.partial(join_kernel, own.shape[0]),
        out_shape=[shape] * 2,
        grid=(1,),
        in_specs=[pl.BlockSpec(memory_space=pltpu.SMEM), anywhere, anywhere],
        out_specs=[pl.BlockSpec(own.shape, lambda i: (0, 0, 0, 0))] * 2,
        scratch_shapes=[pltpu.SemaphoreType.DMA((2, 2))],
    )(scalars, own, other)


def source_kernel(parts, freqs, dirs, rows, low, size, lean, cuts, scalars, gain_ref, drop_ref,
                  along_ref, across_ref, *refs):
    count = parts + (4 if lean else 2 * parts)
    ins, outs = refs[:count], refs[count : count + parts * cuts]
    (window, wind, back_up, back_down, centre, post, in_sems, out_sems) = refs[
        count + parts * cuts :
    ]
    spot = scalars[SPOT]
    even = scalars[EVEN]
    first = scalars[GROUP_FIRST]
    span = parts * freqs
    step = sub_rows(size)
    pieces = size // step

    def block_of(turn):
        return lax.rem(spot + parts - turn, parts)

    def fetches(piece):
        moves = [(ins[turn], 0, freqs, HERE * span + block_of(turn) * freqs) for turn in range(parts)]
        for side in range(2):
            above = even if side == 0 else 1 - even
            base = above * (ABOVE * span)
            if lean:
                near, rest = ins[parts + 2 * side], ins[parts + 2 * side + 1]
                skip = 1 - above
                moves += [
                    (near, 0, freqs - 1, base + spot * freqs + skip),
                    (rest, skip, freqs - 1, base + (1 - spot) * freqs + skip),
                    (rest, above * (freqs - 1), 1, base + freqs - above),
                ]
            else:
                moves += [
                    (ins[parts * (1 + side) + turn], 0, freqs, base + block_of(turn) * freqs)
                    for turn in range(parts)
                ]
        return [
            pltpu.make_async_copy(
                ref.at[pl.ds(start, length), :, pl.ds(piece * step, step), :],
                window.at[piece, pl.ds(place, length)],
                in_sems.at[piece, index],
            )
            for index, (ref, start, length, place) in enumerate(moves)
        ]

    share = freqs // cuts

    def stores(piece):
        return [
            pltpu.make_async_copy(
                post.at[piece, pl.ds(block_of(turn) * freqs + cut * share, share)],
                outs[turn * cuts + cut].at[:, :, pl.ds(piece * step, step), :],
                out_sems.at[piece, turn * cuts + cut],
            )
            for turn in range(parts)
            for cut in range(cuts)
        ]

    for piece in range(pieces):
        for copy in fetches(piece):
            copy.start()

    scale_up = TRANSFER_FACTOR * WEIGHT_UPPER
    scale_down = TRANSFER_FACTOR * WEIGHT_LOWER
    cross = TRANSFER_FACTOR * WEIGHT_CROSS / (scale_up * scale_down)
    near = taps(ANGLE_NEAR * dirs / 360.0)
    far = taps(ANGLE_FAR * dirs / 360.0)

    starts = [b * rows + low for b in range(parts)]
    along = pick([along_ref[s : s + size, :] for s in starts], spot)
    across = pick([across_ref[s : s + size, :] for s in starts], spot)

    for piece in range(pieces):
        at = piece * step
        for j in range(dirs):
            angle = 2.0 * math.pi * j / dirs
            wind[j] = along[at : at + step] * math.cos(angle) + across[at : at + step] * math.sin(angle)
        for copy in fetches(piece):
            copy.wait()

        for flag, group in ((HAS_BELOW, BELOW), (HAS_ABOVE, ABOVE)):

            @pl.when(scalars[flag] == 0)
            def _(group=group):
                def clear(f, carry):
                    window[piece, group * span + f] = jnp.zeros(window.shape[2:], jnp.float32)
                    return carry

                lax.fori_loop(0, span, clear, 0)

        def delta_step(index, carry):
            k = span - REACH_HIGH + index

            @functools.cache
            def energy(j):
                return window[piece, k, j]

            @functools.cache
            def upper(j):
                (o0, w0), (o1, w1) = UP_TAPS
                return (scale_up * w0) * window[piece, k + o0, j] + (scale_up * w1) * window[
                    piece, k + o1, j
                ]

            @functools.cache
            def lower(j):
                (o0, w0), (o1, w1) = DOWN_TAPS
                return (scale_down * w0) * window[piece, k + o0, j] + (scale_down * w1) * window[
                    piece, k + o1, j
                ]

            @functools.cache
            def delta(sign, j):
                plus = sum(w * upper((j + sign * o) % dirs) for o, w in near)
                minus = sum(w * lower((j - sign * o) % dirs) for o, w in far)
                value = energy(j)
                return value * (value * (plus + minus) - cross * (plus * minus))

            for j in range(dirs):
                back_up[index, j] = sum(
                    w * (delta(1, (j - o) % dirs) + delta(-1, (j + o) % dirs)) for o, w in near
                )
                back_down[index, j] = sum(
                    w * (delta(1, (j + o) % dirs) + delta(-1, (j - o) % dirs)) for o, w in far
                )
                centre[index, j] = -2.0 * (delta(1, j) + delta(-1, j))
            return carry

        lax.fori_loop(0, span + REACH, delta_step, 0)

        def out_step(m, carry):
            gain = gain_ref[first + m]
            drop = drop_ref[first + m]
            index = m + REACH_HIGH
            for j in range(dirs):
                value = window[piece, span + m, j]
                total = value * (1.0 + jnp.maximum(0.0, gain * wind[j] - drop)) + centre[index, j]
                for o, w in UP_TAPS:
                    total = total + w * back_up[index - o, j]
                for o, w in DOWN_TAPS:
                    total = total + w * back_down[index - o, j]
                post[piece, m, j] = total
            return carry

        lax.fori_loop(0, span, out_step, 0)
        for copy in stores(piece):
            copy.start()
    for piece in range(pieces):
        for copy in stores(piece):
            copy.wait()


def source(scalars, gain, drop, along, across, operands, chunk, parts, freqs, lean, cuts):
    column, low, size = chunk
    dirs = operands[0].shape[1]
    total_rows = along.shape[0]
    rows = total_rows // parts
    span = parts * freqs
    step = sub_rows(size)
    pieces = size // step
    shape = jax.ShapeDtypeStruct((freqs // cuts, dirs, size, LANES), jnp.float32)
    smem = pl.BlockSpec(memory_space=pltpu.SMEM)
    anywhere = pl.BlockSpec(memory_space=pl.ANY)
    wind_spec = pl.BlockSpec((total_rows, LANES), lambda i: (0, column))
    inner = (dirs, step, LANES)
    return pl.pallas_call(
        functools.partial(source_kernel, parts, freqs, dirs, rows, low, size, lean, cuts),
        out_shape=[shape] * (parts * cuts),
        grid=(1,),
        in_specs=[smem, smem, smem, wind_spec, wind_spec] + [anywhere] * len(operands),
        out_specs=[anywhere] * (parts * cuts),
        scratch_shapes=[
            pltpu.VMEM((pieces, 3 * span) + inner, jnp.float32),
            pltpu.VMEM(inner, jnp.float32),
            pltpu.VMEM((span + REACH,) + inner, jnp.float32),
            pltpu.VMEM((span + REACH,) + inner, jnp.float32),
            pltpu.VMEM((span + REACH,) + inner, jnp.float32),
            pltpu.VMEM((pieces, span) + inner, jnp.float32),
            pltpu.SemaphoreType.DMA((pieces, parts + 2 * max(3, parts))),
            pltpu.SemaphoreType.DMA((pieces, parts * cuts)),
        ],
        compiler_params=pltpu.CompilerParams(vmem_limit_bytes=VMEM_LIMIT),
    )(scalars, gain, drop, along, across, *operands)


def face_weights(courant, forward):
    curve = (courant * courant - 1.0) * (1.0 / 6.0)
    half = 0.5 * courant
    if forward:
        return (courant * curve, courant * (0.5 + half - 2.0 * curve), courant * (0.5 - half + curve))
    return (courant * (0.5 + half + curve), courant * (0.5 - half - 2.0 * curve), courant * curve)


EDGE = 8


def sweep_kernel(parts, layout, dirs, rows, start, aliased, scalars, speed_ref, cos_ref, sin_ref,
                 geo_ref, mask_ref, *refs):
    tiles = len(layout) - 2
    count = sum(len(pieces) for pieces in layout) * parts
    ins = refs[:count]
    out_ref, buffer = refs[count + aliased :]
    spot = scalars[SPOT]
    total_rows = rows * parts
    speed = speed_ref[scalars[OWN_FIRST] + start + pl.program_id(0)]
    lane = lax.broadcasted_iota(jnp.int32, (total_rows, LANES), 1)
    row_zero = jnp.zeros((EDGE, LANES), jnp.float32)
    slots = buffer.shape[0]
    for slot in range(slots):
        for tile in range(tiles):
            buffer[slot, tile, :EDGE] = row_zero
            buffer[slot, tile, EDGE + total_rows :] = row_zero

    def column(tile, j):
        at = sum(len(pieces) for pieces in layout[:tile]) * parts
        pieces = []
        for index in range(len(layout[tile])):
            blocks = [ins[at + index * parts + turn][0, j] for turn in range(parts)]
            pieces.append([pick(blocks, lax.rem(b + parts - spot, parts)) for b in range(parts)])
        return jnp.concatenate([piece[b] for b in range(parts) for piece in pieces], axis=0)

    def one(j, forward, northward, slot):
        cells = [column(tile, j) for tile in range(tiles + 2)]
        weights = face_weights((speed * cos_ref[j]) * geo_ref[0], forward)
        moved = [pltpu.roll(cell, 1, axis=1) for cell in cells]
        steps = [cells[0] - moved[0]]
        for tile in range(1, tiles + 2):
            steps.append(cells[tile] - jnp.where(lane < 1, moved[tile - 1], moved[tile]))

        def ahead(amount):
            turned = [None] + [pltpu.roll(step, LANES - amount, axis=1) for step in steps[1:]]
            return [None] + [
                jnp.where(lane >= LANES - amount, turned[tile + 1], turned[tile])
                for tile in range(1, tiles + 1)
            ]

        if forward:
            turned = [pltpu.roll(step, 1, axis=1) for step in steps[:-1]]
            rear = [None] + [
                jnp.where(lane < 1, turned[tile - 1], turned[tile]) for tile in range(1, tiles + 1)
            ]
            spread = (rear, steps, ahead(1))
        else:
            spread = (steps, ahead(1), ahead(2))
        low, mid, high = face_weights(speed * sin_ref[j], northward)
        for tile in range(tiles):
            here = slice(tile * LANES, (tile + 1) * LANES)
            mask = mask_ref[:, here].astype(jnp.float32)
            swept = cells[tile + 1]
            for weight, value in zip(weights, spread):
                swept = swept - weight * value[tile + 1]
            swept = swept * mask
            buffer[slot, tile, EDGE : EDGE + total_rows] = swept

            def shifted(amount, tile=tile):
                return buffer[slot, tile, EDGE + amount : EDGE + amount + total_rows]

            under, over = shifted(-1), shifted(1)
            if northward:
                front = low * under + mid * swept + high * over
                rear_flux = low * shifted(-2) + mid * under + high * swept
            else:
                front = low * swept + mid * over + high * shifted(2)
                rear_flux = low * under + mid * swept + high * over
            out_ref[0, j, :, here] = (swept - geo_ref[1] * front + geo_ref[2] * rear_flux) * mask

    angles = [2.0 * math.pi * j / dirs for j in range(dirs)]
    kinds = [(round(math.cos(angle), 12) >= 0.0, round(math.sin(angle), 12) >= 0.0) for angle in angles]
    begin = 0
    while begin < dirs:
        end = begin
        while end < dirs and kinds[end] == kinds[begin]:
            end += 1
        kind = kinds[begin]
        whole = (end - begin) // slots

        def body(index, carry, kind=kind, begin=begin):
            for slot in range(slots):
                one(begin + index * slots + slot, *kind, slot)
            return carry

        lax.fori_loop(0, whole, body, 0)
        for j in range(begin + whole * slots, end):
            one(j, *kind, 0)
        begin = end


def sweep(scalars, speed, cosines, sines, geometry, sea_mask, layout, start, length, freqs, result):
    parts = len(layout[0][0])
    total_rows, width = sea_mask.shape
    dirs = cosines.shape[0]
    rows = total_rows // parts
    flat = [entry for pieces in layout for piece in pieces for entry in piece]
    smem = pl.BlockSpec(memory_space=pltpu.SMEM)

    def block(array, origin):
        offset = start - origin
        return pl.BlockSpec((1,) + array.shape[1:], lambda f: (f + offset, 0, 0, 0))

    operands = [array for array, _ in flat]
    specs = [block(array, origin) for array, origin in flat]
    aliases = {}
    if result is not None:
        aliases = {6 + len(operands): 0}
        operands.append(result)
        specs.append(pl.BlockSpec(memory_space=pl.ANY))
    return pl.pallas_call(
        functools.partial(
            sweep_kernel, parts, [[None] * len(pieces) for pieces in layout], dirs, rows, start,
            len(aliases),
        ),
        out_shape=jax.ShapeDtypeStruct((freqs, dirs, total_rows, width), jnp.float32),
        grid=(length,),
        in_specs=[smem] * 4
        + [
            pl.BlockSpec((3, total_rows, LANES), lambda f: (0, 0, 0)),
            pl.BlockSpec((total_rows, width), lambda f: (0, 0)),
        ]
        + specs,
        out_specs=pl.BlockSpec((1, dirs, total_rows, width), lambda f: (f + start, 0, 0, 0)),
        scratch_shapes=[
            pltpu.VMEM((2, width // LANES, total_rows + 2 * EDGE, LANES), jnp.float32)
        ],
        input_output_aliases=aliases,
        compiler_params=pltpu.CompilerParams(vmem_limit_bytes=VMEM_LIMIT),
    )(scalars, speed, cosines, sines, geometry, sea_mask, *operands)


def group_size(comp_count, freq_local, band_rows):
    for parts in range(1, comp_count + 1):
        if comp_count % parts == 0 and band_rows % parts == 0 and parts * freq_local >= REACH:
            return parts
    return comp_count


def chunk_list(tiles, rows):
    columns = [tiles - 1] + list(range(tiles - 1))
    chunks = [(column, 0, rows) for column in columns]
    if rows % 16 == 0:
        column = columns[-1]
        chunks[-1:] = [(column, 0, rows // 2), (column, rows // 2, rows // 2)]
    return chunks


def shards(spectra, u_wind, wind_dir, sea_mask):
    freq_local, band_rows, dir_count, lon_cells = spectra.shape
    comp_count = lax.axis_size("comp")
    grid_count = lax.axis_size("grid")
    parts = group_size(comp_count, freq_local, band_rows)
    lean = parts == 2
    groups = comp_count // parts
    comp_index = lax.axis_index("comp")
    spot = lax.rem(comp_index, parts)
    group = lax.div(comp_index, parts)
    scalars = jnp.stack(
        [
            spot,
            group * (parts * freq_local),
            comp_index * freq_local,
            1 - lax.rem(group, 2),
            (group > 0).astype(jnp.int32),
            (group < groups - 1).astype(jnp.int32),
        ]
    ).astype(jnp.int32)

    turns = []
    for turn in range(parts):
        turns.append([(i, i - i % parts + (i % parts + turn) % parts) for i in range(comp_count)])
    returns = [[(target, origin) for origin, target in pairs] for pairs in turns]

    def partners(other):
        pairs = []
        for g in range(grid_count):
            for i in range(comp_count):
                mate = other(i // parts)
                if 0 <= mate < groups:
                    target = g * comp_count + mate * parts + i % parts
                else:
                    target = (g ^ 1 if g ^ 1 < grid_count else g) * comp_count + i
                pairs.append((g * comp_count + i, target))
        return pairs

    sides = [partners(lambda g: g + 1 - 2 * (g % 2)), partners(lambda g: g - 1 + 2 * (g % 2))]
    eastward = [(i, i + 1) for i in range(grid_count - 1)]
    westward = [(i + 1, i) for i in range(grid_count - 1)]

    omega = 2.0 * math.pi * FREQ_LOW * FREQ_RATIO ** np.arange(freq_local * comp_count)
    factor = WIND_FACTOR * SOURCE_STEP
    gain = jnp.asarray(factor * omega * omega / GRAVITY, jnp.float32)
    drop = jnp.asarray(factor * omega, jnp.float32)
    speed = jnp.asarray(
        GRAVITY / (2.0 * omega) * ADVECT_STEP / (EARTH_RADIUS * CELL_RADIANS), jnp.float32
    )
    angles = 2.0 * math.pi * np.arange(dir_count) / dir_count
    cosines = jnp.asarray(np.cos(angles), jnp.float32)
    sines = jnp.asarray(np.sin(angles), jnp.float32)
    cells = np.cos(
        np.radians(BAND_CENTRE + (np.arange(band_rows) - (band_rows - 1) / 2.0) * CELL_DEGREES)
    )
    faces = np.cos(
        np.radians(BAND_CENTRE + (np.arange(band_rows + 1) - band_rows / 2.0) * CELL_DEGREES)
    )
    geometry = np.stack([1.0 / cells, faces[1:] / cells, faces[:-1] / cells])
    geometry = jnp.asarray(np.repeat(geometry[:, :, None], LANES, axis=2), jnp.float32)

    along = u_wind * jnp.cos(wind_dir)
    across = u_wind * jnp.sin(wind_dir)

    field = jnp.transpose(spectra, (0, 2, 1, 3))
    tiles = lon_cells // LANES
    rows = band_rows // parts
    chunks = chunk_list(tiles, rows)
    halves = 2 if freq_local % 2 == 0 else 1
    half = freq_local // halves

    both = ("grid", "comp")

    done = [[] for _ in range(tiles)]
    for index, chunk in enumerate(chunks):
        packed = pack(scalars, field, sea_mask, chunk, parts, lean)
        held = [packed[0]] + [
            lax.ppermute(packed[turn], "comp", turns[turn]) for turn in range(1, parts)
        ]
        operands = list(held)
        if lean:
            joined = join(scalars, held[0], held[1])
            for side, pairs in enumerate(sides):
                operands.append(lax.ppermute(packed[parts + side], both, pairs))
                operands.append(lax.ppermute(joined[side], both, pairs))
        else:
            for pairs in sides:
                for turn in range(parts):
                    operands.append(lax.ppermute(held[turn], both, pairs))
        cuts = halves if index == len(chunks) - 1 else 1
        post = source(
            scalars, gain, drop, along, across, operands, chunk, parts, freq_local, lean, cuts
        )
        piece = []
        for turn in range(parts):
            own = list(post[turn * cuts : (turn + 1) * cuts])
            if turn > 0:
                own = [lax.ppermute(value, "comp", returns[turn]) for value in own]
            piece.append(own)
        done[chunk[0]].append(piece)

    def border(column, pairs):
        return [
            [[lax.ppermute(value, "grid", pairs) for value in cuts] for cuts in piece]
            for piece in done[column]
        ]

    layout = [border(tiles - 1, eastward)] + done + [border(0, westward)]
    result = None
    for part in range(halves):
        entries = [
            [
                [
                    (cuts[part], part * half) if len(cuts) > 1 else (cuts[0], 0)
                    for cuts in piece
                ]
                for piece in pieces
            ]
            for pieces in layout
        ]
        result = sweep(
            scalars, speed, cosines, sines, geometry, sea_mask, entries, part * half, half,
            freq_local, result,
        )
    return jnp.transpose(result, (0, 2, 1, 3))


def solution(mesh):
    return jax.shard_map(
        shards,
        mesh=mesh,
        in_specs=(P("comp", None, None, "grid"), P(None, "grid"), P(None, "grid"), P(None, "grid")),
        out_specs=P("comp", None, None, "grid"),
        check_vma=False,
    )
```

```python
import functools
import math

import jax
import jax.numpy as jnp
import numpy as np
from jax import lax
from jax.experimental import pallas as pl
from jax.experimental.pallas import tpu as pltpu
from jax.sharding import PartitionSpec as P


GRAVITY = 9.81
FREQ_LOW = 0.04
FREQ_RATIO = 1.1
LAMBDA = 0.25
SOURCE_STEP = 120.0
ADVECT_STEP = 220.0
WIND_FACTOR = 0.0003125
TRANSFER_FACTOR = 0.1
EARTH_RADIUS = 6371000.0
BAND_CENTRE = 30.0
CELL_DEGREES = 0.05
CELL_RADIANS = CELL_DEGREES * math.pi / 180.0
ANGLE_NEAR = 11.48
ANGLE_FAR = 33.56
FREQ_UPPER_SHIFT = math.log(1.0 + LAMBDA) / math.log(FREQ_RATIO)
FREQ_LOWER_SHIFT = math.log(1.0 - LAMBDA) / math.log(FREQ_RATIO)
WEIGHT_UPPER = 1.0 / (1.0 + LAMBDA) ** 4
WEIGHT_LOWER = 1.0 / (1.0 - LAMBDA) ** 4
WEIGHT_CROSS = 2.0 / (1.0 - LAMBDA * LAMBDA) ** 4

LANES = 128
VMEM_LIMIT = 60 * 1024 * 1024


def taps(shift):
    low = math.floor(shift)
    part = shift - low
    return ((low, 1.0 - part), (low + 1, part))


UP_TAPS = taps(FREQ_UPPER_SHIFT)
DOWN_TAPS = taps(FREQ_LOWER_SHIFT)
REACH_HIGH = UP_TAPS[1][0]
REACH_LOW = -DOWN_TAPS[0][0]
REACH = REACH_HIGH + REACH_LOW


def pick(values, index):
    chosen = values[0]
    for place in range(1, len(values)):
        chosen = jnp.where(index == place, values[place], chosen)
    return chosen


def sub_rows(rows):
    return 8 if rows % 8 == 0 else rows


SPOT, GROUP_FIRST, OWN_FIRST, EVEN, HAS_BELOW, HAS_ABOVE = range(6)
BELOW, HERE, ABOVE = range(3)


def pack_kernel(parts, rows, low, size, lean, scalars, x_ref, mask_ref, *outs):
    spot = scalars[SPOT]
    freqs = x_ref.shape[0]
    for turn in range(parts):
        block = lax.rem(spot + turn, parts)
        if size % 8 == 0:
            here = pl.ds(pl.multiple_of(block * rows + low, 8), size)
            mask = mask_ref[here].astype(jnp.float32)
            for f in range(freqs):
                outs[turn][f] = x_ref[f, :, here, :] * mask[None]
        else:
            spots = [slice(b * rows + low, b * rows + low + size) for b in range(parts)]
            mask = pick([mask_ref[here] for here in spots], block).astype(jnp.float32)
            for f in range(freqs):
                outs[turn][f] = pick([x_ref[f, :, here, :] for here in spots], block) * mask[None]
    if lean:
        even = scalars[EVEN]
        outs[parts][...] = outs[0][pl.ds(even, freqs - 1)]
        outs[parts + 1][...] = outs[0][pl.ds(1 - even, freqs - 1)]


def pack(scalars, spectra, sea_mask, chunk, parts, lean):
    column, low, size = chunk
    freqs, dirs, total_rows, _ = spectra.shape
    rows = total_rows // parts

    def shape(count):
        return jax.ShapeDtypeStruct((count, dirs, size, LANES), jnp.float32)

    counts = [freqs] * parts + [freqs - 1] * (2 if lean else 0)
    return pl.pallas_call(
        functools.partial(pack_kernel, parts, rows, low, size, lean),
        out_shape=[shape(count) for count in counts],
        grid=(1,),
        in_specs=[
            pl.BlockSpec(memory_space=pltpu.SMEM),
            pl.BlockSpec((freqs, dirs, total_rows, LANES), lambda i: (0, 0, 0, column)),
            pl.BlockSpec((total_rows, LANES), lambda i: (0, column)),
        ],
        out_specs=[
            pl.BlockSpec((count, dirs, size, LANES), lambda i: (0, 0, 0, 0)) for count in counts
        ],
        compiler_params=pltpu.CompilerParams(vmem_limit_bytes=VMEM_LIMIT),
    )(scalars, spectra, sea_mask)


def join_kernel(freqs, scalars, own_ref, other_ref, a_ref, b_ref, sems):
    even, spot = scalars[EVEN], scalars[SPOT]
    for side, (out_ref, up) in enumerate(((a_ref, even), (b_ref, 1 - even))):
        rest = pltpu.make_async_copy(
            other_ref.at[pl.ds(up, freqs - 1)], out_ref.at[pl.ds(up, freqs - 1)], sems.at[side, 0]
        )
        rest.start()
        place = (1 - up) * (freqs - 1)
        from_own = spot == up

        @pl.when(from_own)
        def _():
            pltpu.make_async_copy(own_ref.at[place], out_ref.at[place], sems.at[side, 1]).start()

        @pl.when(jnp.logical_not(from_own))
        def _():
            pltpu.make_async_copy(other_ref.at[place], out_ref.at[place], sems.at[side, 1]).start()

    for side, out_ref in enumerate((a_ref, b_ref)):
        pltpu.make_async_copy(
            other_ref.at[pl.ds(0, freqs - 1)], out_ref.at[pl.ds(0, freqs - 1)], sems.at[side, 0]
        ).wait()
        pltpu.make_async_copy(other_ref.at[0], out_ref.at[0], sems.at[side, 1]).wait()


def join(scalars, own, other):
    anywhere = pl.BlockSpec(memory_space=pl.ANY)
    shape = jax.ShapeDtypeStruct(own.shape, own.dtype)
    return pl.pallas_call(
        functools.partial(join_kernel, own.shape[0]),
        out_shape=[shape] * 2,
        grid=(1,),
        in_specs=[pl.BlockSpec(memory_space=pltpu.SMEM), anywhere, anywhere],
        out_specs=[pl.BlockSpec(own.shape, lambda i: (0, 0, 0, 0))] * 2,
        scratch_shapes=[pltpu.SemaphoreType.DMA((2, 2))],
    )(scalars, own, other)


def source_kernel(parts, freqs, dirs, rows, low, size, lean, cuts, scalars, gain_ref, drop_ref,
                  along_ref, across_ref, *refs):
    count = parts + (4 if lean else 2 * parts)
    ins, outs = refs[:count], refs[count : count + parts * cuts]
    (window, wind, back_up, back_down, centre, post, in_sems, out_sems) = refs[
        count + parts * cuts :
    ]
    spot = scalars[SPOT]
    even = scalars[EVEN]
    first = scalars[GROUP_FIRST]
    span = parts * freqs
    step = sub_rows(size)
    pieces = size // step

    def block_of(turn):
        return lax.rem(spot + parts - turn, parts)

    def fetches(piece):
        moves = [(ins[turn], 0, freqs, HERE * span + block_of(turn) * freqs) for turn in range(parts)]
        for side in range(2):
            above = even if side == 0 else 1 - even
            base = above * (ABOVE * span)
            if lean:
                near, rest = ins[parts + 2 * side], ins[parts + 2 * side + 1]
                skip = 1 - above
                moves += [
                    (near, 0, freqs - 1, base + spot * freqs + skip),
                    (rest, skip, freqs - 1, base + (1 - spot) * freqs + skip),
                    (rest, above * (freqs - 1), 1, base + freqs - above),
                ]
            else:
                moves += [
                    (ins[parts * (1 + side) + turn], 0, freqs, base + block_of(turn) * freqs)
                    for turn in range(parts)
                ]
        return [
            pltpu.make_async_copy(
                ref.at[pl.ds(start, length), :, pl.ds(piece * step, step), :],
                window.at[piece, pl.ds(place, length)],
                in_sems.at[piece, index],
            )
            for index, (ref, start, length, place) in enumerate(moves)
        ]

    share = freqs // cuts

    def stores(piece):
        return [
            pltpu.make_async_copy(
                post.at[piece, pl.ds(block_of(turn) * freqs + cut * share, share)],
                outs[turn * cuts + cut].at[:, :, pl.ds(piece * step, step), :],
                out_sems.at[piece, turn * cuts + cut],
            )
            for turn in range(parts)
            for cut in range(cuts)
        ]

    for piece in range(pieces):
        for copy in fetches(piece):
            copy.start()

    scale_up = TRANSFER_FACTOR * WEIGHT_UPPER
    scale_down = TRANSFER_FACTOR * WEIGHT_LOWER
    cross = TRANSFER_FACTOR * WEIGHT_CROSS / (scale_up * scale_down)
    near = taps(ANGLE_NEAR * dirs / 360.0)
    far = taps(ANGLE_FAR * dirs / 360.0)

    starts = [b * rows + low for b in range(parts)]
    along = pick([along_ref[s : s + size, :] for s in starts], spot)
    across = pick([across_ref[s : s + size, :] for s in starts], spot)

    for piece in range(pieces):
        at = piece * step
        for j in range(dirs):
            angle = 2.0 * math.pi * j / dirs
            wind[j] = along[at : at + step] * math.cos(angle) + across[at : at + step] * math.sin(angle)
        for copy in fetches(piece):
            copy.wait()

        for flag, group in ((HAS_BELOW, BELOW), (HAS_ABOVE, ABOVE)):

            @pl.when(scalars[flag] == 0)
            def _(group=group):
                def clear(f, carry):
                    window[piece, group * span + f] = jnp.zeros(window.shape[2:], jnp.float32)
                    return carry

                lax.fori_loop(0, span, clear, 0)

        def delta_step(index, carry):
            k = span - REACH_HIGH + index

            @functools.cache
            def energy(j):
                return window[piece, k, j]

            @functools.cache
            def upper(j):
                (o0, w0), (o1, w1) = UP_TAPS
                return (scale_up * w0) * window[piece, k + o0, j] + (scale_up * w1) * window[
                    piece, k + o1, j
                ]

            @functools.cache
            def lower(j):
                (o0, w0), (o1, w1) = DOWN_TAPS
                return (scale_down * w0) * window[piece, k + o0, j] + (scale_down * w1) * window[
                    piece, k + o1, j
                ]

            @functools.cache
            def delta(sign, j):
                plus = sum(w * upper((j + sign * o) % dirs) for o, w in near)
                minus = sum(w * lower((j - sign * o) % dirs) for o, w in far)
                value = energy(j)
                return value * (value * (plus + minus) - cross * (plus * minus))

            for j in range(dirs):
                back_up[index, j] = sum(
                    w * (delta(1, (j - o) % dirs) + delta(-1, (j + o) % dirs)) for o, w in near
                )
                back_down[index, j] = sum(
                    w * (delta(1, (j + o) % dirs) + delta(-1, (j - o) % dirs)) for o, w in far
                )
                centre[index, j] = -2.0 * (delta(1, j) + delta(-1, j))
            return carry

        lax.fori_loop(0, span + REACH, delta_step, 0)

        def out_step(m, carry):
            gain = gain_ref[first + m]
            drop = drop_ref[first + m]
            index = m + REACH_HIGH
            for j in range(dirs):
                value = window[piece, span + m, j]
                total = value * (1.0 + jnp.maximum(0.0, gain * wind[j] - drop)) + centre[index, j]
                for o, w in UP_TAPS:
                    total = total + w * back_up[index - o, j]
                for o, w in DOWN_TAPS:
                    total = total + w * back_down[index - o, j]
                post[piece, m, j] = total
            return carry

        lax.fori_loop(0, span, out_step, 0)
        for copy in stores(piece):
            copy.start()
    for piece in range(pieces):
        for copy in stores(piece):
            copy.wait()


def source(scalars, gain, drop, along, across, operands, chunk, parts, freqs, lean, cuts):
    column, low, size = chunk
    dirs = operands[0].shape[1]
    total_rows = along.shape[0]
    rows = total_rows // parts
    span = parts * freqs
    step = sub_rows(size)
    pieces = size // step
    shape = jax.ShapeDtypeStruct((freqs // cuts, dirs, size, LANES), jnp.float32)
    smem = pl.BlockSpec(memory_space=pltpu.SMEM)
    anywhere = pl.BlockSpec(memory_space=pl.ANY)
    wind_spec = pl.BlockSpec((total_rows, LANES), lambda i: (0, column))
    inner = (dirs, step, LANES)
    return pl.pallas_call(
        functools.partial(source_kernel, parts, freqs, dirs, rows, low, size, lean, cuts),
        out_shape=[shape] * (parts * cuts),
        grid=(1,),
        in_specs=[smem, smem, smem, wind_spec, wind_spec] + [anywhere] * len(operands),
        out_specs=[anywhere] * (parts * cuts),
        scratch_shapes=[
            pltpu.VMEM((pieces, 3 * span) + inner, jnp.float32),
            pltpu.VMEM(inner, jnp.float32),
            pltpu.VMEM((span + REACH,) + inner, jnp.float32),
            pltpu.VMEM((span + REACH,) + inner, jnp.float32),
            pltpu.VMEM((span + REACH,) + inner, jnp.float32),
            pltpu.VMEM((pieces, span) + inner, jnp.float32),
            pltpu.SemaphoreType.DMA((pieces, parts + 2 * max(3, parts))),
            pltpu.SemaphoreType.DMA((pieces, parts * cuts)),
        ],
        compiler_params=pltpu.CompilerParams(vmem_limit_bytes=VMEM_LIMIT),
    )(scalars, gain, drop, along, across, *operands)


def face_weights(courant, forward):
    curve = (courant * courant - 1.0) * (1.0 / 6.0)
    half = 0.5 * courant
    if forward:
        return (courant * curve, courant * (0.5 + half - 2.0 * curve), courant * (0.5 - half + curve))
    return (courant * (0.5 + half + curve), courant * (0.5 - half - 2.0 * curve), courant * curve)


EDGE = 8
INVERSE, AHEAD, BEHIND, AHEAD_NOT_FIRST, BEHIND_NOT_FIRST, BEHIND_NOT_FIRST_TWO = range(6)
AHEAD_NOT_LAST, BEHIND_NOT_LAST, AHEAD_NOT_LAST_TWO = range(6, 9)


def cell_weights(courant):
    def combine(forward):
        low, mid, high = face_weights(courant, forward)
        if forward:
            return (low, mid - low, 1.0 - mid + high, -high)
        return (low, 1.0 - low + mid, high - mid, -high)

    return combine


def sweep_kernel(parts, layout, dirs, rows, start, aliased, scalars, speed_ref, cos_ref, sin_ref,
                 geo_ref, mask_ref, *refs):
    tiles = len(layout) - 2
    count = sum(len(pieces) for pieces in layout) * parts
    ins = refs[:count]
    out_ref, buffer, mask = refs[count + aliased :]
    spot = scalars[SPOT]
    total_rows = rows * parts
    speed = speed_ref[scalars[OWN_FIRST] + start + pl.program_id(0)]
    step = sub_rows(rows // max(len(pieces) for pieces in layout))
    lane = lax.broadcasted_iota(jnp.int32, (step, LANES), 1)
    slots = buffer.shape[0]

    @pl.when((pl.program_id(0) == 0) & (pl.program_id(1) == 0))
    def _():
        mask[...] = mask_ref[...].astype(jnp.float32)
        edge = jnp.zeros((EDGE, LANES), jnp.float32)
        for slot in range(slots):
            for tile in range(tiles):
                buffer[slot, tile, :EDGE] = edge
                buffer[slot, tile, EDGE + total_rows :] = edge

    def cell(tile, block, low, j):
        at = sum(len(pieces) for pieces in layout[:tile]) * parts
        length = rows // len(layout[tile])
        piece, inside = divmod(low, length)
        held = ins[at + piece * parts : at + (piece + 1) * parts]
        if step % 8 == 0:
            return held[block][0, j, inside : inside + step]
        turn = lax.rem(block + parts - spot, parts)
        return pick([ref[0, j, inside : inside + step] for ref in held], turn)

    def along_longitude(j, base, forward, slot):
        for block in range(parts):
            for low in range(0, rows, step):
                if step % 8 == 0:
                    place = pl.multiple_of(lax.rem(spot + block, parts) * rows + low, 8)
                else:
                    place = block * rows + low
                cells = [cell(tile, block, low, j) for tile in range(tiles + 2)]
                courant = (speed * cos_ref[base + j]) * geo_ref[INVERSE, pl.ds(place, step)]
                weights = cell_weights(courant)(forward)

                def shifted(amount):
                    if amount == 0:
                        return cells[1:-1]
                    used = cells[:-1] if amount < 0 else [None] + cells[1:]
                    turned = [
                        value if value is None else pltpu.roll(value, -amount % LANES, axis=1)
                        for value in used
                    ]
                    if amount < 0:
                        return [
                            jnp.where(lane < -amount, turned[tile - 1], turned[tile])
                            for tile in range(1, tiles + 1)
                        ]
                    return [
                        jnp.where(lane >= LANES - amount, turned[tile + 1], turned[tile])
                        for tile in range(1, tiles + 1)
                    ]

                spread = [shifted(amount) for amount in ((-2, -1, 0, 1) if forward else (-1, 0, 1, 2))]
                for tile in range(tiles):
                    swept = sum(weight * value[tile] for weight, value in zip(weights, spread))
                    swept = swept * mask[pl.ds(place, step), tile * LANES : (tile + 1) * LANES]
                    buffer[slot, tile, pl.ds(EDGE + place, step)] = swept

    def along_latitude(j, base, northward, slot):
        low, mid, high = face_weights(speed * sin_ref[base + j], northward)
        block = sub_rows(total_rows)
        for row in range(0, total_rows, block):
            here = slice(row, row + block)
            if northward:
                weights = (
                    low * geo_ref[BEHIND_NOT_FIRST_TWO, here],
                    mid * geo_ref[BEHIND_NOT_FIRST, here] - low * geo_ref[AHEAD_NOT_FIRST, here],
                    1.0 - mid * geo_ref[AHEAD, here] + high * geo_ref[BEHIND, here],
                    -high * geo_ref[AHEAD_NOT_LAST, here],
                )
            else:
                weights = (
                    low * geo_ref[BEHIND_NOT_FIRST, here],
                    1.0 - low * geo_ref[AHEAD, here] + mid * geo_ref[BEHIND, here],
                    high * geo_ref[BEHIND_NOT_LAST, here] - mid * geo_ref[AHEAD_NOT_LAST, here],
                    -high * geo_ref[AHEAD_NOT_LAST_TWO, here],
                )
            for tile in range(tiles):
                total = 0.0
                for amount, weight in zip((-2, -1, 0, 1) if northward else (-1, 0, 1, 2), weights):
                    at = EDGE + row + amount
                    total = total + weight * buffer[slot, tile, at : at + block]
                across = slice(tile * LANES, (tile + 1) * LANES)
                out_ref[0, j, here, across] = total * mask[here, across]

    def quarter(forward, northward):
        base = pl.program_id(1) * dirs

        for j in range(dirs + 1):
            if j < dirs:
                along_longitude(j, base, forward, j % slots)
            if j > 0:
                along_latitude(j - 1, base, northward, (j - 1) % slots)

    for index, kind in enumerate(((True, True), (False, True), (False, False), (True, False))):
        pl.when(pl.program_id(1) == index)(functools.partial(quarter, *kind))


def sweep(scalars, speed, cosines, sines, geometry, sea_mask, layout, start, length, freqs, result):
    parts = len(layout[0][0])
    total_rows, width = sea_mask.shape
    dirs = cosines.shape[0]
    rows = total_rows // parts
    flat = [entry for pieces in layout for piece in pieces for entry in piece]
    smem = pl.BlockSpec(memory_space=pltpu.SMEM)

    quarter = dirs // 4

    def block(array, origin):
        offset = start - origin
        shape = (1, quarter) + array.shape[2:]
        return pl.BlockSpec(shape, lambda f, q: (f + offset, q, 0, 0))

    operands = [array for array, _ in flat]
    specs = [block(array, origin) for array, origin in flat]
    aliases = {}
    if result is not None:
        aliases = {6 + len(operands): 0}
        operands.append(result)
        specs.append(pl.BlockSpec(memory_space=pl.ANY))
    return pl.pallas_call(
        functools.partial(
            sweep_kernel, parts, [[None] * len(pieces) for pieces in layout], quarter, rows, start,
            len(aliases),
        ),
        out_shape=jax.ShapeDtypeStruct((freqs, dirs, total_rows, width), jnp.float32),
        grid=(length, 4),
        in_specs=[smem] * 4
        + [
            pl.BlockSpec(geometry.shape, lambda f, q: (0, 0, 0)),
            pl.BlockSpec((total_rows, width), lambda f, q: (0, 0)),
        ]
        + specs,
        out_specs=pl.BlockSpec((1, quarter, total_rows, width), lambda f, q: (f + start, q, 0, 0)),
        scratch_shapes=[
            pltpu.VMEM((3, width // LANES, total_rows + 2 * EDGE, LANES), jnp.float32),
            pltpu.VMEM((total_rows, width), jnp.float32),
        ],
        input_output_aliases=aliases,
        compiler_params=pltpu.CompilerParams(vmem_limit_bytes=VMEM_LIMIT),
    )(scalars, speed, cosines, sines, geometry, sea_mask, *operands)


def group_size(comp_count, freq_local, band_rows):
    for parts in range(1, comp_count + 1):
        if comp_count % parts == 0 and band_rows % parts == 0 and parts * freq_local >= REACH:
            return parts
    return comp_count


def chunk_list(tiles, rows):
    columns = [tiles - 1] + list(range(tiles - 1))
    chunks = [(column, 0, rows) for column in columns]
    if rows % 16 == 0:
        column = columns[-1]
        chunks[-1:] = [(column, 0, rows // 2), (column, rows // 2, rows // 2)]
    return chunks


def shards(spectra, u_wind, wind_dir, sea_mask):
    freq_local, band_rows, dir_count, lon_cells = spectra.shape
    comp_count = lax.axis_size("comp")
    grid_count = lax.axis_size("grid")
    parts = group_size(comp_count, freq_local, band_rows)
    lean = parts == 2
    groups = comp_count // parts
    comp_index = lax.axis_index("comp")
    spot = lax.rem(comp_index, parts)
    group = lax.div(comp_index, parts)
    scalars = jnp.stack(
        [
            spot,
            group * (parts * freq_local),
            comp_index * freq_local,
            1 - lax.rem(group, 2),
            (group > 0).astype(jnp.int32),
            (group < groups - 1).astype(jnp.int32),
        ]
    ).astype(jnp.int32)

    turns = []
    for turn in range(parts):
        turns.append([(i, i - i % parts + (i % parts + turn) % parts) for i in range(comp_count)])
    returns = [[(target, origin) for origin, target in pairs] for pairs in turns]

    def partners(other):
        pairs = []
        for g in range(grid_count):
            for i in range(comp_count):
                mate = other(i // parts)
                if 0 <= mate < groups:
                    target = g * comp_count + mate * parts + i % parts
                else:
                    target = (g ^ 1 if g ^ 1 < grid_count else g) * comp_count + i
                pairs.append((g * comp_count + i, target))
        return pairs

    sides = [partners(lambda g: g + 1 - 2 * (g % 2)), partners(lambda g: g - 1 + 2 * (g % 2))]
    eastward = [(i, i + 1) for i in range(grid_count - 1)]
    westward = [(i + 1, i) for i in range(grid_count - 1)]

    omega = 2.0 * math.pi * FREQ_LOW * FREQ_RATIO ** np.arange(freq_local * comp_count)
    factor = WIND_FACTOR * SOURCE_STEP
    gain = jnp.asarray(factor * omega * omega / GRAVITY, jnp.float32)
    drop = jnp.asarray(factor * omega, jnp.float32)
    speed = jnp.asarray(
        GRAVITY / (2.0 * omega) * ADVECT_STEP / (EARTH_RADIUS * CELL_RADIANS), jnp.float32
    )
    angles = 2.0 * math.pi * np.arange(dir_count) / dir_count
    cosines = jnp.asarray(np.cos(angles), jnp.float32)
    sines = jnp.asarray(np.sin(angles), jnp.float32)
    cells = np.cos(
        np.radians(BAND_CENTRE + (np.arange(band_rows) - (band_rows - 1) / 2.0) * CELL_DEGREES)
    )
    faces = np.cos(
        np.radians(BAND_CENTRE + (np.arange(band_rows + 1) - band_rows / 2.0) * CELL_DEGREES)
    )
    ahead, behind = faces[1:] / cells, faces[:-1] / cells
    place = np.arange(band_rows)
    not_first, not_last = place > 0, place < band_rows - 1
    geometry = np.stack(
        [
            1.0 / cells,
            ahead,
            behind,
            ahead * not_first,
            behind * not_first,
            behind * (place > 1),
            ahead * not_last,
            behind * not_last,
            ahead * (place < band_rows - 2),
        ]
    )
    geometry = jnp.asarray(np.repeat(geometry[:, :, None], LANES, axis=2), jnp.float32)

    along = u_wind * jnp.cos(wind_dir)
    across = u_wind * jnp.sin(wind_dir)

    field = jnp.transpose(spectra, (0, 2, 1, 3))
    tiles = lon_cells // LANES
    rows = band_rows // parts
    chunks = chunk_list(tiles, rows)
    halves = 2 if freq_local % 2 == 0 else 1
    half = freq_local // halves

    both = ("grid", "comp")

    done = [[] for _ in range(tiles)]
    for index, chunk in enumerate(chunks):
        packed = pack(scalars, field, sea_mask, chunk, parts, lean)
        held = [packed[0]] + [
            lax.ppermute(packed[turn], "comp", turns[turn]) for turn in range(1, parts)
        ]
        operands = list(held)
        if lean:
            joined = join(scalars, held[0], held[1])
            for side, pairs in enumerate(sides):
                operands.append(lax.ppermute(packed[parts + side], both, pairs))
                operands.append(lax.ppermute(joined[side], both, pairs))
        else:
            for pairs in sides:
                for turn in range(parts):
                    operands.append(lax.ppermute(held[turn], both, pairs))
        cuts = halves if index == len(chunks) - 1 else 1
        post = source(
            scalars, gain, drop, along, across, operands, chunk, parts, freq_local, lean, cuts
        )
        piece = []
        for turn in range(parts):
            own = list(post[turn * cuts : (turn + 1) * cuts])
            if turn > 0:
                own = [lax.ppermute(value, "comp", returns[turn]) for value in own]
            piece.append(own)
        done[chunk[0]].append(piece)

    def border(column, pairs):
        return [
            [[lax.ppermute(value, "grid", pairs) for value in cuts] for cuts in piece]
            for piece in done[column]
        ]

    layout = [border(tiles - 1, eastward)] + done + [border(0, westward)]
    result = None
    for part in range(halves):
        entries = [
            [
                [
                    (cuts[part], part * half) if len(cuts) > 1 else (cuts[0], 0)
                    for cuts in piece
                ]
                for piece in pieces
            ]
            for pieces in layout
        ]
        result = sweep(
            scalars, speed, cosines, sines, geometry, sea_mask, entries, part * half, half,
            freq_local, result,
        )
    return jnp.transpose(result, (0, 2, 1, 3))


def solution(mesh):
    return jax.shard_map(
        shards,
        mesh=mesh,
        in_specs=(P("comp", None, None, "grid"), P(None, "grid"), P(None, "grid"), P(None, "grid")),
        out_specs=P("comp", None, None, "grid"),
        check_vma=False,
    )
```

```python
import functools
import math

import jax
import jax.numpy as jnp
import numpy as np
from jax import lax
from jax.experimental import pallas as pl
from jax.experimental.pallas import tpu as pltpu
from jax.sharding import PartitionSpec as P


GRAVITY = 9.81
FREQ_LOW = 0.04
FREQ_RATIO = 1.1
LAMBDA = 0.25
SOURCE_STEP = 120.0
ADVECT_STEP = 220.0
WIND_FACTOR = 0.0003125
TRANSFER_FACTOR = 0.1
EARTH_RADIUS = 6371000.0
BAND_CENTRE = 30.0
CELL_DEGREES = 0.05
CELL_RADIANS = CELL_DEGREES * math.pi / 180.0
ANGLE_NEAR = 11.48
ANGLE_FAR = 33.56
FREQ_UPPER_SHIFT = math.log(1.0 + LAMBDA) / math.log(FREQ_RATIO)
FREQ_LOWER_SHIFT = math.log(1.0 - LAMBDA) / math.log(FREQ_RATIO)
WEIGHT_UPPER = 1.0 / (1.0 + LAMBDA) ** 4
WEIGHT_LOWER = 1.0 / (1.0 - LAMBDA) ** 4
WEIGHT_CROSS = 2.0 / (1.0 - LAMBDA * LAMBDA) ** 4

LANES = 128
VMEM_LIMIT = 60 * 1024 * 1024


def taps(shift):
    low = math.floor(shift)
    part = shift - low
    return ((low, 1.0 - part), (low + 1, part))


UP_TAPS = taps(FREQ_UPPER_SHIFT)
DOWN_TAPS = taps(FREQ_LOWER_SHIFT)
REACH_HIGH = UP_TAPS[1][0]
REACH_LOW = -DOWN_TAPS[0][0]
REACH = REACH_HIGH + REACH_LOW


def pick(values, index):
    chosen = values[0]
    for place in range(1, len(values)):
        chosen = jnp.where(index == place, values[place], chosen)
    return chosen


def sub_rows(rows):
    return 8 if rows % 8 == 0 else rows


SPOT, GROUP_FIRST, OWN_FIRST, EVEN, HAS_BELOW, HAS_ABOVE = range(6)
BELOW, HERE, ABOVE = range(3)


def pack_kernel(parts, rows, low, size, lean, scalars, x_ref, mask_ref, *outs):
    spot = scalars[SPOT]
    freqs = x_ref.shape[0]
    for turn in range(parts):
        block = lax.rem(spot + turn, parts)
        if size % 8 == 0:
            here = pl.ds(pl.multiple_of(block * rows + low, 8), size)
            mask = mask_ref[here].astype(jnp.float32)
            for f in range(freqs):
                outs[turn][f] = x_ref[f, :, here, :] * mask[None]
        else:
            spots = [slice(b * rows + low, b * rows + low + size) for b in range(parts)]
            mask = pick([mask_ref[here] for here in spots], block).astype(jnp.float32)
            for f in range(freqs):
                outs[turn][f] = pick([x_ref[f, :, here, :] for here in spots], block) * mask[None]
    if lean:
        even = scalars[EVEN]
        outs[parts][...] = outs[0][pl.ds(even, freqs - 1)]
        outs[parts + 1][...] = outs[0][pl.ds(1 - even, freqs - 1)]


def pack(scalars, spectra, sea_mask, chunk, parts, lean):
    column, low, size = chunk
    freqs, dirs, total_rows, _ = spectra.shape
    rows = total_rows // parts

    def shape(count):
        return jax.ShapeDtypeStruct((count, dirs, size, LANES), jnp.float32)

    counts = [freqs] * parts + [freqs - 1] * (2 if lean else 0)
    return pl.pallas_call(
        functools.partial(pack_kernel, parts, rows, low, size, lean),
        out_shape=[shape(count) for count in counts],
        grid=(1,),
        in_specs=[
            pl.BlockSpec(memory_space=pltpu.SMEM),
            pl.BlockSpec((freqs, dirs, total_rows, LANES), lambda i: (0, 0, 0, column)),
            pl.BlockSpec((total_rows, LANES), lambda i: (0, column)),
        ],
        out_specs=[
            pl.BlockSpec((count, dirs, size, LANES), lambda i: (0, 0, 0, 0)) for count in counts
        ],
        compiler_params=pltpu.CompilerParams(vmem_limit_bytes=VMEM_LIMIT),
    )(scalars, spectra, sea_mask)


def join_kernel(freqs, scalars, own_ref, other_ref, a_ref, b_ref, sems):
    even, spot = scalars[EVEN], scalars[SPOT]
    for side, (out_ref, up) in enumerate(((a_ref, even), (b_ref, 1 - even))):
        rest = pltpu.make_async_copy(
            other_ref.at[pl.ds(up, freqs - 1)], out_ref.at[pl.ds(up, freqs - 1)], sems.at[side, 0]
        )
        rest.start()
        place = (1 - up) * (freqs - 1)
        from_own = spot == up

        @pl.when(from_own)
        def _():
            pltpu.make_async_copy(own_ref.at[place], out_ref.at[place], sems.at[side, 1]).start()

        @pl.when(jnp.logical_not(from_own))
        def _():
            pltpu.make_async_copy(other_ref.at[place], out_ref.at[place], sems.at[side, 1]).start()

    for side, out_ref in enumerate((a_ref, b_ref)):
        pltpu.make_async_copy(
            other_ref.at[pl.ds(0, freqs - 1)], out_ref.at[pl.ds(0, freqs - 1)], sems.at[side, 0]
        ).wait()
        pltpu.make_async_copy(other_ref.at[0], out_ref.at[0], sems.at[side, 1]).wait()


def join(scalars, own, other):
    anywhere = pl.BlockSpec(memory_space=pl.ANY)
    shape = jax.ShapeDtypeStruct(own.shape, own.dtype)
    return pl.pallas_call(
        functools.partial(join_kernel, own.shape[0]),
        out_shape=[shape] * 2,
        grid=(1,),
        in_specs=[pl.BlockSpec(memory_space=pltpu.SMEM), anywhere, anywhere],
        out_specs=[pl.BlockSpec(own.shape, lambda i: (0, 0, 0, 0))] * 2,
        scratch_shapes=[pltpu.SemaphoreType.DMA((2, 2))],
    )(scalars, own, other)


def source_kernel(parts, freqs, dirs, rows, low, size, lean, cuts, scalars, gain_ref, drop_ref,
                  along_ref, across_ref, *refs):
    count = parts + (4 if lean else 2 * parts)
    ins, outs = refs[:count], refs[count : count + parts * cuts]
    (window, wind, back_up, back_down, centre, post, in_sems, out_sems) = refs[
        count + parts * cuts :
    ]
    spot = scalars[SPOT]
    even = scalars[EVEN]
    first = scalars[GROUP_FIRST]
    span = parts * freqs
    step = sub_rows(size)
    pieces = size // step

    def block_of(turn):
        return lax.rem(spot + parts - turn, parts)

    def fetches(piece):
        moves = [(ins[turn], 0, freqs, HERE * span + block_of(turn) * freqs) for turn in range(parts)]
        for side in range(2):
            above = even if side == 0 else 1 - even
            base = above * (ABOVE * span)
            if lean:
                near, rest = ins[parts + 2 * side], ins[parts + 2 * side + 1]
                skip = 1 - above
                moves += [
                    (near, 0, freqs - 1, base + spot * freqs + skip),
                    (rest, skip, freqs - 1, base + (1 - spot) * freqs + skip),
                    (rest, above * (freqs - 1), 1, base + freqs - above),
                ]
            else:
                moves += [
                    (ins[parts * (1 + side) + turn], 0, freqs, base + block_of(turn) * freqs)
                    for turn in range(parts)
                ]
        return [
            pltpu.make_async_copy(
                ref.at[pl.ds(start, length), :, pl.ds(piece * step, step), :],
                window.at[piece, pl.ds(place, length)],
                in_sems.at[piece, index],
            )
            for index, (ref, start, length, place) in enumerate(moves)
        ]

    share = freqs // cuts

    def stores(piece):
        return [
            pltpu.make_async_copy(
                post.at[piece, pl.ds(block_of(turn) * freqs + cut * share, share)],
                outs[turn * cuts + cut].at[:, :, pl.ds(piece * step, step), :],
                out_sems.at[piece, turn * cuts + cut],
            )
            for turn in range(parts)
            for cut in range(cuts)
        ]

    for piece in range(pieces):
        for copy in fetches(piece):
            copy.start()

    scale_up = TRANSFER_FACTOR * WEIGHT_UPPER
    scale_down = TRANSFER_FACTOR * WEIGHT_LOWER
    cross = TRANSFER_FACTOR * WEIGHT_CROSS / (scale_up * scale_down)
    near = taps(ANGLE_NEAR * dirs / 360.0)
    far = taps(ANGLE_FAR * dirs / 360.0)

    starts = [b * rows + low for b in range(parts)]
    along = pick([along_ref[s : s + size, :] for s in starts], spot)
    across = pick([across_ref[s : s + size, :] for s in starts], spot)

    for piece in range(pieces):
        at = piece * step
        for j in range(dirs):
            angle = 2.0 * math.pi * j / dirs
            wind[j] = along[at : at + step] * math.cos(angle) + across[at : at + step] * math.sin(angle)
        for copy in fetches(piece):
            copy.wait()

        for flag, group in ((HAS_BELOW, BELOW), (HAS_ABOVE, ABOVE)):

            @pl.when(scalars[flag] == 0)
            def _(group=group):
                def clear(f, carry):
                    window[piece, group * span + f] = jnp.zeros(window.shape[2:], jnp.float32)
                    return carry

                lax.fori_loop(0, span, clear, 0)

        def delta_step(index, carry):
            k = span - REACH_HIGH + index

            @functools.cache
            def energy(j):
                return window[piece, k, j]

            @functools.cache
            def upper(j):
                (o0, w0), (o1, w1) = UP_TAPS
                return (scale_up * w0) * window[piece, k + o0, j] + (scale_up * w1) * window[
                    piece, k + o1, j
                ]

            @functools.cache
            def lower(j):
                (o0, w0), (o1, w1) = DOWN_TAPS
                return (scale_down * w0) * window[piece, k + o0, j] + (scale_down * w1) * window[
                    piece, k + o1, j
                ]

            @functools.cache
            def delta(sign, j):
                plus = sum(w * upper((j + sign * o) % dirs) for o, w in near)
                minus = sum(w * lower((j - sign * o) % dirs) for o, w in far)
                value = energy(j)
                return value * (value * (plus + minus) - cross * (plus * minus))

            for j in range(dirs):
                back_up[index, j] = sum(
                    w * (delta(1, (j - o) % dirs) + delta(-1, (j + o) % dirs)) for o, w in near
                )
                back_down[index, j] = sum(
                    w * (delta(1, (j + o) % dirs) + delta(-1, (j - o) % dirs)) for o, w in far
                )
                centre[index, j] = -2.0 * (delta(1, j) + delta(-1, j))
            return carry

        lax.fori_loop(0, span + REACH, delta_step, 0)

        def out_step(m, carry):
            gain = gain_ref[first + m]
            drop = drop_ref[first + m]
            index = m + REACH_HIGH
            for j in range(dirs):
                value = window[piece, span + m, j]
                total = value * (1.0 + jnp.maximum(0.0, gain * wind[j] - drop)) + centre[index, j]
                for o, w in UP_TAPS:
                    total = total + w * back_up[index - o, j]
                for o, w in DOWN_TAPS:
                    total = total + w * back_down[index - o, j]
                post[piece, m, j] = total
            return carry

        lax.fori_loop(0, span, out_step, 0)
        for copy in stores(piece):
            copy.start()
    for piece in range(pieces):
        for copy in stores(piece):
            copy.wait()


def source(scalars, gain, drop, along, across, operands, chunk, parts, freqs, lean, cuts):
    column, low, size = chunk
    dirs = operands[0].shape[1]
    total_rows = along.shape[0]
    rows = total_rows // parts
    span = parts * freqs
    step = sub_rows(size)
    pieces = size // step
    shape = jax.ShapeDtypeStruct((freqs // cuts, dirs, size, LANES), jnp.float32)
    smem = pl.BlockSpec(memory_space=pltpu.SMEM)
    anywhere = pl.BlockSpec(memory_space=pl.ANY)
    wind_spec = pl.BlockSpec((total_rows, LANES), lambda i: (0, column))
    inner = (dirs, step, LANES)
    return pl.pallas_call(
        functools.partial(source_kernel, parts, freqs, dirs, rows, low, size, lean, cuts),
        out_shape=[shape] * (parts * cuts),
        grid=(1,),
        in_specs=[smem, smem, smem, wind_spec, wind_spec] + [anywhere] * len(operands),
        out_specs=[anywhere] * (parts * cuts),
        scratch_shapes=[
            pltpu.VMEM((pieces, 3 * span) + inner, jnp.float32),
            pltpu.VMEM(inner, jnp.float32),
            pltpu.VMEM((span + REACH,) + inner, jnp.float32),
            pltpu.VMEM((span + REACH,) + inner, jnp.float32),
            pltpu.VMEM((span + REACH,) + inner, jnp.float32),
            pltpu.VMEM((pieces, span) + inner, jnp.float32),
            pltpu.SemaphoreType.DMA((pieces, parts + 2 * max(3, parts))),
            pltpu.SemaphoreType.DMA((pieces, parts * cuts)),
        ],
        compiler_params=pltpu.CompilerParams(vmem_limit_bytes=VMEM_LIMIT),
    )(scalars, gain, drop, along, across, *operands)


def face_weights(courant, forward):
    curve = (courant * courant - 1.0) * (1.0 / 6.0)
    half = 0.5 * courant
    if forward:
        return (courant * curve, courant * (0.5 + half - 2.0 * curve), courant * (0.5 - half + curve))
    return (courant * (0.5 + half + curve), courant * (0.5 - half - 2.0 * curve), courant * curve)


EDGE = 8
INVERSE, AHEAD, BEHIND, AHEAD_NOT_FIRST, BEHIND_NOT_FIRST, BEHIND_NOT_FIRST_TWO = range(6)
AHEAD_NOT_LAST, BEHIND_NOT_LAST, AHEAD_NOT_LAST_TWO = range(6, 9)


def cell_weights(courant):
    def combine(forward):
        low, mid, high = face_weights(courant, forward)
        if forward:
            return (low, mid - low, 1.0 - mid + high, -high)
        return (low, 1.0 - low + mid, high - mid, -high)

    return combine


def sweep_kernel(parts, layout, dirs, rows, start, aliased, scalars, speed_ref, cos_ref, sin_ref,
                 geo_ref, mask_ref, *refs):
    tiles = len(layout) - 2
    count = sum(len(pieces) for pieces in layout) * parts
    ins = refs[:count]
    out_ref, buffer, mask = refs[count + aliased :]
    spot = scalars[SPOT]
    total_rows = rows * parts
    speed = speed_ref[scalars[OWN_FIRST] + start + pl.program_id(0)]
    step = sub_rows(rows // max(len(pieces) for pieces in layout))
    lane = lax.broadcasted_iota(jnp.int32, (step, LANES), 1)
    slots = buffer.shape[0]

    @pl.when((pl.program_id(0) == 0) & (pl.program_id(1) == 0))
    def _():
        mask[...] = mask_ref[...].astype(jnp.float32)
        edge = jnp.zeros((EDGE, LANES), jnp.float32)
        for slot in range(slots):
            for tile in range(tiles):
                buffer[slot, tile, :EDGE] = edge
                buffer[slot, tile, EDGE + total_rows :] = edge

    def cell(tile, block, low, j):
        at = sum(len(pieces) for pieces in layout[:tile]) * parts
        length = rows // len(layout[tile])
        piece, inside = divmod(low, length)
        held = ins[at + piece * parts : at + (piece + 1) * parts]
        if step % 8 == 0:
            return held[block][0, j, inside : inside + step]
        turn = lax.rem(block + parts - spot, parts)
        return pick([ref[0, j, inside : inside + step] for ref in held], turn)

    def along_longitude(j, base, forward, slot):
        for block in range(parts):
            for low in range(0, rows, step):
                if step % 8 == 0:
                    place = pl.multiple_of(lax.rem(spot + block, parts) * rows + low, 8)
                else:
                    place = block * rows + low
                cells = [cell(tile, block, low, j) for tile in range(tiles + 2)]
                courant = (speed * cos_ref[base + j]) * geo_ref[INVERSE, pl.ds(place, step)]
                weights = cell_weights(courant)(forward)

                def shifted(amount):
                    if amount == 0:
                        return cells[1:-1]
                    used = cells[:-1] if amount < 0 else [None] + cells[1:]
                    turned = [
                        value if value is None else pltpu.roll(value, -amount % LANES, axis=1)
                        for value in used
                    ]
                    if amount < 0:
                        return [
                            jnp.where(lane < -amount, turned[tile - 1], turned[tile])
                            for tile in range(1, tiles + 1)
                        ]
                    return [
                        jnp.where(lane >= LANES - amount, turned[tile + 1], turned[tile])
                        for tile in range(1, tiles + 1)
                    ]

                spread = [shifted(amount) for amount in ((-2, -1, 0, 1) if forward else (-1, 0, 1, 2))]
                for tile in range(tiles):
                    swept = sum(weight * value[tile] for weight, value in zip(weights, spread))
                    swept = swept * mask[pl.ds(place, step), tile * LANES : (tile + 1) * LANES]
                    buffer[slot, tile, pl.ds(EDGE + place, step)] = swept

    def along_latitude(j, base, northward, slot):
        low, mid, high = face_weights(speed * sin_ref[base + j], northward)
        block = sub_rows(total_rows)
        for row in range(0, total_rows, block):
            here = slice(row, row + block)
            if northward:
                weights = (
                    low * geo_ref[BEHIND_NOT_FIRST_TWO, here],
                    mid * geo_ref[BEHIND_NOT_FIRST, here] - low * geo_ref[AHEAD_NOT_FIRST, here],
                    1.0 - mid * geo_ref[AHEAD, here] + high * geo_ref[BEHIND, here],
                    -high * geo_ref[AHEAD_NOT_LAST, here],
                )
            else:
                weights = (
                    low * geo_ref[BEHIND_NOT_FIRST, here],
                    1.0 - low * geo_ref[AHEAD, here] + mid * geo_ref[BEHIND, here],
                    high * geo_ref[BEHIND_NOT_LAST, here] - mid * geo_ref[AHEAD_NOT_LAST, here],
                    -high * geo_ref[AHEAD_NOT_LAST_TWO, here],
                )
            for tile in range(tiles):
                total = 0.0
                for amount, weight in zip((-2, -1, 0, 1) if northward else (-1, 0, 1, 2), weights):
                    at = EDGE + row + amount
                    total = total + weight * buffer[slot, tile, at : at + block]
                across = slice(tile * LANES, (tile + 1) * LANES)
                out_ref[0, j, here, across] = total * mask[here, across]

    base = pl.program_id(1) * dirs
    share = dirs // 2

    def quarter(begin, forward, northward):
        for j in range(begin, begin + share + 1):
            if j < begin + share:
                along_longitude(j, base, forward, j % slots)
            if j > begin:
                along_latitude(j - 1, base, northward, (j - 1) % slots)

    def northern():
        quarter(0, True, True)
        quarter(share, False, True)

    def southern():
        quarter(0, False, False)
        quarter(share, True, False)

    pl.when(pl.program_id(1) == 0)(northern)
    pl.when(pl.program_id(1) == 1)(southern)


def sweep(scalars, speed, cosines, sines, geometry, sea_mask, layout, start, length, freqs, result):
    parts = len(layout[0][0])
    total_rows, width = sea_mask.shape
    dirs = cosines.shape[0]
    rows = total_rows // parts
    flat = [entry for pieces in layout for piece in pieces for entry in piece]
    smem = pl.BlockSpec(memory_space=pltpu.SMEM)

    half_circle = dirs // 2

    def block(array, origin):
        offset = start - origin
        shape = (1, half_circle) + array.shape[2:]
        return pl.BlockSpec(shape, lambda f, q: (f + offset, q, 0, 0))

    operands = [array for array, _ in flat]
    specs = [block(array, origin) for array, origin in flat]
    aliases = {}
    if result is not None:
        aliases = {6 + len(operands): 0}
        operands.append(result)
        specs.append(pl.BlockSpec(memory_space=pl.ANY))
    return pl.pallas_call(
        functools.partial(
            sweep_kernel, parts, [[None] * len(pieces) for pieces in layout], half_circle, rows, start,
            len(aliases),
        ),
        out_shape=jax.ShapeDtypeStruct((freqs, dirs, total_rows, width), jnp.float32),
        grid=(length, 2),
        in_specs=[smem] * 4
        + [
            pl.BlockSpec(geometry.shape, lambda f, q: (0, 0, 0)),
            pl.BlockSpec((total_rows, width), lambda f, q: (0, 0)),
        ]
        + specs,
        out_specs=pl.BlockSpec((1, half_circle, total_rows, width), lambda f, q: (f + start, q, 0, 0)),
        scratch_shapes=[
            pltpu.VMEM((3, width // LANES, total_rows + 2 * EDGE, LANES), jnp.float32),
            pltpu.VMEM((total_rows, width), jnp.float32),
        ],
        input_output_aliases=aliases,
        compiler_params=pltpu.CompilerParams(vmem_limit_bytes=VMEM_LIMIT),
    )(scalars, speed, cosines, sines, geometry, sea_mask, *operands)


def group_size(comp_count, freq_local, band_rows):
    for parts in range(1, comp_count + 1):
        if comp_count % parts == 0 and band_rows % parts == 0 and parts * freq_local >= REACH:
            return parts
    return comp_count


def chunk_list(tiles, rows):
    columns = [tiles - 1] + list(range(tiles - 1))
    chunks = [(column, 0, rows) for column in columns]
    if rows % 16 == 0:
        column = columns[-1]
        chunks[-1:] = [(column, 0, rows // 2), (column, rows // 2, rows // 2)]
    return chunks


def shards(spectra, u_wind, wind_dir, sea_mask):
    freq_local, band_rows, dir_count, lon_cells = spectra.shape
    comp_count = lax.axis_size("comp")
    grid_count = lax.axis_size("grid")
    parts = group_size(comp_count, freq_local, band_rows)
    lean = parts == 2
    groups = comp_count // parts
    comp_index = lax.axis_index("comp")
    spot = lax.rem(comp_index, parts)
    group = lax.div(comp_index, parts)
    scalars = jnp.stack(
        [
            spot,
            group * (parts * freq_local),
            comp_index * freq_local,
            1 - lax.rem(group, 2),
            (group > 0).astype(jnp.int32),
            (group < groups - 1).astype(jnp.int32),
        ]
    ).astype(jnp.int32)

    turns = []
    for turn in range(parts):
        turns.append([(i, i - i % parts + (i % parts + turn) % parts) for i in range(comp_count)])
    returns = [[(target, origin) for origin, target in pairs] for pairs in turns]

    def partners(other):
        pairs = []
        for g in range(grid_count):
            for i in range(comp_count):
                mate = other(i // parts)
                if 0 <= mate < groups:
                    target = g * comp_count + mate * parts + i % parts
                else:
                    target = (g ^ 1 if g ^ 1 < grid_count else g) * comp_count + i
                pairs.append((g * comp_count + i, target))
        return pairs

    sides = [partners(lambda g: g + 1 - 2 * (g % 2)), partners(lambda g: g - 1 + 2 * (g % 2))]
    eastward = [(i, i + 1) for i in range(grid_count - 1)]
    westward = [(i + 1, i) for i in range(grid_count - 1)]

    omega = 2.0 * math.pi * FREQ_LOW * FREQ_RATIO ** np.arange(freq_local * comp_count)
    factor = WIND_FACTOR * SOURCE_STEP
    gain = jnp.asarray(factor * omega * omega / GRAVITY, jnp.float32)
    drop = jnp.asarray(factor * omega, jnp.float32)
    speed = jnp.asarray(
        GRAVITY / (2.0 * omega) * ADVECT_STEP / (EARTH_RADIUS * CELL_RADIANS), jnp.float32
    )
    angles = 2.0 * math.pi * np.arange(dir_count) / dir_count
    cosines = jnp.asarray(np.cos(angles), jnp.float32)
    sines = jnp.asarray(np.sin(angles), jnp.float32)
    cells = np.cos(
        np.radians(BAND_CENTRE + (np.arange(band_rows) - (band_rows - 1) / 2.0) * CELL_DEGREES)
    )
    faces = np.cos(
        np.radians(BAND_CENTRE + (np.arange(band_rows + 1) - band_rows / 2.0) * CELL_DEGREES)
    )
    ahead, behind = faces[1:] / cells, faces[:-1] / cells
    place = np.arange(band_rows)
    not_first, not_last = place > 0, place < band_rows - 1
    geometry = np.stack(
        [
            1.0 / cells,
            ahead,
            behind,
            ahead * not_first,
            behind * not_first,
            behind * (place > 1),
            ahead * not_last,
            behind * not_last,
            ahead * (place < band_rows - 2),
        ]
    )
    geometry = jnp.asarray(np.repeat(geometry[:, :, None], LANES, axis=2), jnp.float32)

    along = u_wind * jnp.cos(wind_dir)
    across = u_wind * jnp.sin(wind_dir)

    field = jnp.transpose(spectra, (0, 2, 1, 3))
    tiles = lon_cells // LANES
    rows = band_rows // parts
    chunks = chunk_list(tiles, rows)
    halves = 2 if freq_local % 2 == 0 else 1
    half = freq_local // halves

    both = ("grid", "comp")

    done = [[] for _ in range(tiles)]
    for index, chunk in enumerate(chunks):
        packed = pack(scalars, field, sea_mask, chunk, parts, lean)
        held = [packed[0]] + [
            lax.ppermute(packed[turn], "comp", turns[turn]) for turn in range(1, parts)
        ]
        operands = list(held)
        if lean:
            joined = join(scalars, held[0], held[1])
            for side, pairs in enumerate(sides):
                operands.append(lax.ppermute(packed[parts + side], both, pairs))
                operands.append(lax.ppermute(joined[side], both, pairs))
        else:
            for pairs in sides:
                for turn in range(parts):
                    operands.append(lax.ppermute(held[turn], both, pairs))
        cuts = halves if index == len(chunks) - 1 else 1
        post = source(
            scalars, gain, drop, along, across, operands, chunk, parts, freq_local, lean, cuts
        )
        piece = []
        for turn in range(parts):
            own = list(post[turn * cuts : (turn + 1) * cuts])
            if turn > 0:
                own = [lax.ppermute(value, "comp", returns[turn]) for value in own]
            piece.append(own)
        done[chunk[0]].append(piece)

    def border(column, pairs):
        return [
            [[lax.ppermute(value, "grid", pairs) for value in cuts] for cuts in piece]
            for piece in done[column]
        ]

    layout = [border(tiles - 1, eastward)] + done + [border(0, westward)]
    result = None
    for part in range(halves):
        entries = [
            [
                [
                    (cuts[part], part * half) if len(cuts) > 1 else (cuts[0], 0)
                    for cuts in piece
                ]
                for piece in pieces
            ]
            for pieces in layout
        ]
        result = sweep(
            scalars, speed, cosines, sines, geometry, sea_mask, entries, part * half, half,
            freq_local, result,
        )
    return jnp.transpose(result, (0, 2, 1, 3))


def solution(mesh):
    return jax.shard_map(
        shards,
        mesh=mesh,
        in_specs=(P("comp", None, None, "grid"), P(None, "grid"), P(None, "grid"), P(None, "grid")),
        out_specs=P("comp", None, None, "grid"),
        check_vma=False,
    )
```
